32 devices in a mesh: rows: 8 (over y, x, core), cols: 4 (over z).
Axes of the slice: x: 2, y: 2, z: 4, core: 2. Of those that a mesh axis runs over, the one named last changes fastest.
Arguments:
- white_real: float32 [4096, 4096], P('rows', 'cols'), may hold values from -6 to 6
- white_imag: float32 [4096, 4096], P('rows', 'cols'), may hold values from -6 to 6
- covariates: bfloat16 [16, 4096, 4096], P(None, 'rows', 'cols'), may hold values from -6 to 6
- coefficients: float32 [16], replicated, may hold values from -0.9 to 0.9
- counts: int32 [4096, 4096], P('rows', 'cols'), may hold values from 0 to 5
- land_mask: int32 [4096, 4096], P('rows', 'cols'), may hold values from 0 to 1
- field_hyper: float32 [2], replicated, may hold values from 1 to 2
Outputs:
- step_real: float32 [4096, 4096], P('rows', 'cols')
- step_imag: float32 [4096, 4096], P('rows', 'cols')
- coef_grad: float32 [16], replicated
- objective: float32 [], replicated
The draws below stay inside these ranges and needn't reach their ends.
All inputs are finite; a program needn't handle non-finite values.
Results may differ from the reference program's by a relative error of at most 0.0003.
Values sent between devices are 32-bit elements; how exact they have to be, the bound alone decides.
No kernel may reach another device: no remote copies, remote signals or barrier semaphores. Data moves between devices by JAX's collectives and lax.ppermute only.
A program may use at most 128 MiB of HBM per device.

```python
import jax
import jax.numpy as jnp
from jax import lax

NG = 4096
NCOV = 16


def draw_land_mask(key, part):
    block_len = 16
    block_count = NG // block_len
    scores = jax.random.randint(key, (block_count, block_count), 0, 100)
    block_rows = lax.iota(jnp.int32, block_count)
    limits = 25 + 60 * block_rows // max(block_count - 1, 1)
    blocks = (scores < limits[:, None]).astype(jnp.int32)
    return jnp.repeat(jnp.repeat(blocks, block_len, axis=0), block_len, axis=1)


def touch_ends(values, own_key, low, top_value):
    extent = values.shape
    spot = [jax.random.randint(jax.random.fold_in(own_key, axis), (), 0, extent[axis]) for axis in range(len(extent))]
    values = values.at[tuple(spot)].set(low)
    longest = extent.index(max(extent))
    spot[longest] = (spot[longest] + 1) % extent[longest]
    return values.at[tuple(spot)].set(top_value)


def block_levels(own_key, dims, split, low, high):
    factor_of = 1.0
    for axis_at, parts in split:
        steps = jax.random.uniform(jax.random.fold_in(jax.random.fold_in(own_key, 6), axis_at), (parts,), jnp.float32, low / len(split), high / len(split))
        factor_of = factor_of * jnp.repeat(jnp.exp(steps), dims[axis_at] // parts).reshape((-1,) + (1,) * (len(dims) - 1 - axis_at))
    return factor_of


def scatter_about(stream_key, extent, scale, limit, cuts=(), held_as=jnp.bfloat16):
    factor_of = block_levels(stream_key, extent, cuts, -0.22, 0.18) if cuts else 1.0
    values = jax.random.normal(stream_key, extent, jnp.float32) * scale * factor_of
    return jnp.minimum(jnp.maximum(values, -limit), limit).astype(held_as)


def setup_inputs(seed: int = 0) -> dict:
    key_list = jax.random.split(jax.random.key(seed), 8)
    return {
        "white_real": scatter_about(key_list[0], (NG, NG), 1.0, 6.0, ((0, 8), (1, 4)), jnp.float32),
        "white_imag": scatter_about(key_list[1], (NG, NG), 1.0, 6.0, ((0, 8), (1, 4)), jnp.float32),
        "covariates": scatter_about(key_list[2], (NCOV, NG, NG), 1.0, 6.0, ((1, 8), (2, 4))),
        "coefficients": scatter_about(key_list[3], (NCOV,), 0.15, 0.9, (), jnp.float32),
        "counts": touch_ends(jax.random.randint(key_list[4], (NG, NG), 0, 6), jax.random.fold_in(key_list[4], 1), 0, 5).astype(jnp.int32),
        "land_mask": draw_land_mask(jax.random.fold_in(key_list[7], 71), 0),
        "field_hyper": jnp.clip(jax.random.uniform(key_list[6], (2,), jnp.float32, 1.0, 2.0), 1.0, 2.0),
    }


lasso_weight = 0.02
ridge_weight = 0.1


def field_spectrum(field_hyper, wave_row, wave_col):
    amplitude = 0.2 * field_hyper[0]
    freq_range = field_hyper[1]
    radius = (wave_row[:, None] * wave_row[:, None] + wave_col[None, :] * wave_col[None, :]) / (freq_range * freq_range)
    return amplitude * (1.0 + (NG / freq_range) * jnp.power(1.0 + radius, -0.75))


def reference(white_real, white_imag, covariates, coefficients, counts, land_mask, field_hyper):
    highest = lax.Precision.HIGHEST
    index = jnp.arange(NG, dtype=jnp.int32)
    folded = jnp.minimum(index, NG - index).astype(jnp.float32)
    spectrum = field_spectrum(field_hyper, folded, folded)
    shaped = lax.complex(spectrum * white_real, spectrum * white_imag)
    latent = jnp.real(jnp.fft.ifft2(shaped)) * NG
    cov_full = covariates.astype(jnp.float32)
    linear = jnp.einsum('j,jrc->rc', coefficients, cov_full, precision=highest)
    log_rate = linear + latent
    intensity = jnp.exp(log_rate)
    land_vals = land_mask.astype(jnp.float32)
    count_vals = counts.astype(jnp.float32)
    residual = land_vals * (intensity - count_vals)
    coef_sum = jnp.einsum('jrc,rc->j', cov_full, residual, precision=highest)
    loss_sum = jnp.sum(land_vals * (intensity - count_vals * log_rate)) + 0.5 * jnp.sum(white_real * white_real + white_imag * white_imag)
    adjoint = jnp.fft.ifft2(lax.complex(residual, jnp.zeros_like(residual))) * NG
    per_cell = 1.0 / (NG * NG)
    coef_grad = coef_sum * per_cell + lasso_weight * jnp.sign(coefficients) + ridge_weight * coefficients
    objective = loss_sum * per_cell + lasso_weight * jnp.sum(jnp.abs(coefficients)) + 0.5 * ridge_weight * jnp.sum(coefficients * coefficients)
    curvature = 1.0 + spectrum * spectrum
    step_real = (spectrum * jnp.real(adjoint) + white_real) / curvature
    step_imag = (white_imag - spectrum * jnp.imag(adjoint)) / curvature
    return (step_real, step_imag, coef_grad, objective)
```

```python
import math

import jax
import jax.numpy as jnp
import ml_dtypes
import numpy as np
from jax import lax
from jax.experimental import pallas as pl
from jax.experimental.pallas import tpu as pltpu
from jax.sharding import PartitionSpec as P

NG = 4096
LANES = 128
HALF = LANES // 2
RADIX = 16
DENSE = NG // RADIX

lasso_weight = 0.02
ridge_weight = 0.1


def split3(values):
    first = values.astype(ml_dtypes.bfloat16)
    rest = values - first.astype(np.float64)
    second = rest.astype(ml_dtypes.bfloat16)
    rest = rest - second.astype(np.float64)
    return first, second, rest.astype(ml_dtypes.bfloat16)


def dense_table():
    index = np.arange(DENSE)
    angles = (index[:, None] * index[None, :] % DENSE) * (2.0 * np.pi / DENSE)
    one, two, three = split3(np.concatenate([np.cos(angles), np.sin(angles)], axis=0))
    return np.concatenate([one, one, one, two, two, three], axis=1)


def twiddle_table():
    angles = np.arange(DENSE)[:, None] * np.arange(RADIX)[None, :] * (2.0 * np.pi / NG)
    table = np.zeros((DENSE, LANES), np.float32)
    table[:, :RADIX] = np.cos(angles)
    table[:, RADIX : 2 * RADIX] = np.sin(angles)
    return table


def half_sign():
    lane = lax.broadcasted_iota(jnp.int32, (1, LANES), 1)
    return jnp.where(lane < HALF, -1.0, 1.0).astype(jnp.float32)


class Packed:
    def __init__(self, sign):
        self.sign = sign

    def add(self, a, b):
        return a + b

    def sub(self, a, b):
        return a - b

    def turn(self, a):
        return pltpu.roll(a, HALF, 1) * self.sign

    def mul(self, a, c, s):
        return a * c + self.turn(a) * s


class Pairs:
    def add(self, a, b):
        return tuple(y if x is None else x if y is None else x + y for x, y in zip(a, b))

    def sub(self, a, b):
        return tuple((None if y is None else -y) if x is None else x if y is None else x - y for x, y in zip(a, b))

    def turn(self, a):
        return (None if a[1] is None else -a[1], a[0])

    def mul(self, a, c, s):
        re, im = a
        if im is None:
            return (re * c, re * s)
        if re is None:
            return (-(im * s), im * c)
        return (re * c - im * s, re * s + im * c)


def dft4(ops, z):
    even, odd = ops.add(z[0], z[2]), ops.sub(z[0], z[2])
    even2, turned = ops.add(z[1], z[3]), ops.turn(ops.sub(z[1], z[3]))
    return [ops.add(even, even2), ops.add(odd, turned), ops.sub(even, even2), ops.sub(odd, turned)]


def dft16(ops, z):
    columns = []
    for q in range(4):
        column = dft4(ops, [z[4 * p + q] for p in range(4)])
        for u in range(1, 4):
            turns = q * u
            if turns == 4:
                column[u] = ops.turn(column[u])
            elif turns:
                angle = 2.0 * math.pi * turns / RADIX
                column[u] = ops.mul(column[u], math.cos(angle), math.sin(angle))
        columns.append(column)
    out = [None] * RADIX
    for u in range(4):
        for v, value in enumerate(dft4(ops, [columns[q][u] for q in range(4)])):
            out[u + 4 * v] = value
    return out


def dense_product(table, values):
    one = values.astype(jnp.bfloat16)
    rest = values - one.astype(jnp.float32)
    two = rest.astype(jnp.bfloat16)
    three = (rest - two.astype(jnp.float32)).astype(jnp.bfloat16)
    parts = jnp.concatenate([one, two, three], axis=0)

    def dot(left, right):
        return jnp.dot(left, right, preferred_element_type=jnp.float32)

    small = dot(table[:, 5 * DENSE :], parts[:DENSE]) + dot(table[:, 3 * DENSE : 5 * DENSE], parts[: 2 * DENSE])
    return small + dot(table[:, : 3 * DENSE], parts)


def spectrum_of(hyper, first_row, first_col, shape):
    rows = lax.broadcasted_iota(jnp.int32, shape, 0) + first_row
    cols = lax.broadcasted_iota(jnp.int32, shape, 1) + first_col
    wave_row = jnp.minimum(rows, NG - rows).astype(jnp.float32)
    wave_col = jnp.minimum(cols, NG - cols).astype(jnp.float32)
    amplitude = 0.2 * hyper[0]
    span = hyper[1]
    base = 1.0 + (wave_row * wave_row + wave_col * wave_col) * (1.0 / (span * span))
    return amplitude * (1.0 + (NG / span) / jnp.sqrt(base * jnp.sqrt(base)))


def scale_kernel(count, place, hyper, real_ref, imag_ref, *outs):
    height = real_ref.shape[0]
    width = real_ref.shape[1]
    me, first_row, first_col = place[0], place[1], place[2]
    squares_ref = outs[-1]
    lane = lax.broadcasted_iota(jnp.int32, (1, LANES), 1)
    low = lane < HALF
    step = 64
    squares_ref[...] = jnp.zeros_like(squares_ref)
    for k in range(count):
        other = jnp.bitwise_xor(me, k)
        start = pl.multiple_of(other * LANES, LANES)

        def body(i, carry, k=k, start=start):
            row = pl.multiple_of(i * step, step)
            real = real_ref[pl.ds(row, step), pl.ds(start, LANES)]
            imag = imag_ref[pl.ds(row, step), pl.ds(start, LANES)]
            spec = spectrum_of(hyper, first_row + row, first_col + start, (step, LANES))
            squares = (real * real + imag * imag).reshape(step // 8, 8, LANES)
            squares_ref[...] += jnp.sum(squares, axis=0)
            real, imag = spec * real, spec * imag
            outs[k][pl.ds(row, step), :] = jnp.where(low, real, pltpu.roll(imag, HALF, 1))
            outs[count + k][pl.ds(row, step), :] = jnp.where(low, pltpu.roll(real, HALF, 1), imag)
            return carry

        lax.fori_loop(0, height // step, body, 0)


def first_axis_kernel(n_in, n_out, place, table_ref, twiddle_ref, *refs):
    ins, outs, (work, done) = refs[:n_in], refs[n_in : n_in + n_out], refs[n_in + n_out :]
    me = place[0]
    sign = half_sign()
    ops = Packed(sign)
    if n_in > 1:
        height = ins[0].shape[0]
        for k in range(n_in):
            start = pl.multiple_of(jnp.bitwise_xor(me, k) * height, height)
            work[pl.ds(start, height), :] = ins[k][...]
        source = work
    else:
        source = ins[0]
    target = done if n_out > 1 else outs[0]
    step = 16

    def butterflies(i, carry):
        row = pl.multiple_of(i * step, step)
        z = dft16(ops, [source[pl.ds(row + DENSE * a, step), :] for a in range(RADIX)])
        factors = twiddle_ref[pl.ds(row, step), :]
        work[pl.ds(row, step), :] = z[0]
        for x in range(1, RADIX):
            cos = jnp.broadcast_to(factors[:, x : x + 1], (step, LANES))
            sin = jnp.broadcast_to(factors[:, RADIX + x : RADIX + x + 1], (step, LANES))
            work[pl.ds(row + DENSE * x, step), :] = ops.mul(z[x], cos, sin)
        return carry

    lax.fori_loop(0, DENSE // step, butterflies, 0)

    def products(p, carry):
        row = pl.multiple_of(p * 2 * DENSE, 2 * DENSE)
        values = jnp.concatenate([work[pl.ds(row, DENSE), :], work[pl.ds(row + DENSE, DENSE), :]], axis=1)
        both = dense_product(table_ref, values)
        for h in range(2):
            lanes = slice(h * LANES, (h + 1) * LANES)
            value = both[:DENSE, lanes] + ops.turn(both[DENSE:, lanes])
            target[pl.ds(2 * p + h, DENSE, stride=RADIX), :] = value
        return carry

    lax.fori_loop(0, RADIX // 2, products, 0)
    if n_out > 1:
        height = outs[0].shape[0]
        for k in range(n_out):
            start = pl.multiple_of(jnp.bitwise_xor(me, k) * height, height)
            outs[k][...] = done[pl.ds(start, height), :]


def second_axis_kernel(n_rows, n_cols, place, table_ref, twiddle_ref, *refs):
    ins, outs, (real, imag, done) = refs[:2], refs[2 : 2 + n_cols], refs[2 + n_cols :]
    me = place[1]
    for r in range(n_rows):
        for c in range(n_cols):
            for j in range(2):
                turned = ins[j][r * n_cols + c].T
                row = (c * n_rows + r) * LANES + j * HALF
                real[row : row + HALF, :] = turned[:HALF]
                imag[row : row + HALF, :] = turned[HALF:]
    ops = Pairs()
    step = 8

    def butterflies(i, carry):
        row = pl.multiple_of(i * step, step)
        where = [pl.ds(row + DENSE * a, step) for a in range(RADIX)]
        z = dft16(ops, [(real[at, :], imag[at, :]) for at in where])
        factors = twiddle_ref[pl.ds(row, step), :]
        for x in range(RADIX):
            value = z[x]
            if x:
                cos = jnp.broadcast_to(factors[:, x : x + 1], (step, LANES))
                sin = jnp.broadcast_to(factors[:, RADIX + x : RADIX + x + 1], (step, LANES))
                value = ops.mul(value, cos, sin)
            real[where[x], :], imag[where[x], :] = value
        return carry

    lax.fori_loop(0, DENSE // step, butterflies, 0)

    def products(p, carry):
        row = pl.multiple_of(p * 2 * DENSE, 2 * DENSE)
        here = [pl.ds(row, DENSE), pl.ds(row + DENSE, DENSE)]
        one = dense_product(table_ref.at[:DENSE], jnp.concatenate([real[at, :] for at in here], axis=1))
        two = dense_product(table_ref.at[DENSE:], jnp.concatenate([imag[at, :] for at in here], axis=1))
        both = one - two
        for h in range(2):
            done[pl.ds(2 * p + h, DENSE, stride=RADIX), :] = both[:, h * LANES : (h + 1) * LANES]
        return carry

    lax.fori_loop(0, RADIX // 2, products, 0)
    width = NG // n_cols
    for k in range(n_cols):
        start = jnp.bitwise_xor(me, k) * width
        for t in range(width // LANES):
            tile = done[pl.ds(pl.multiple_of(start + t * LANES, LANES), LANES), :]
            outs[k][:, t * LANES : (t + 1) * LANES] = tile.T


def second_axis_back_kernel(n_rows, n_cols, place, table_ref, twiddle_ref, *refs):
    ins, outs, (real, imag, real_out, imag_out) = refs[:n_cols], refs[n_cols : n_cols + 2], refs[n_cols + 2 :]
    me = place[1]
    width = NG // n_cols
    for k in range(n_cols):
        start = jnp.bitwise_xor(me, k) * width
        for t in range(width // LANES):
            tile = ins[k][:, t * LANES : (t + 1) * LANES].T
            real[pl.ds(pl.multiple_of(start + t * LANES, LANES), LANES), :] = tile
    ops = Pairs()
    step = 8

    def butterflies(i, carry):
        row = pl.multiple_of(i * step, step)
        where = [pl.ds(row + DENSE * a, step) for a in range(RADIX)]
        z = dft16(ops, [(real[at, :], None) for at in where])
        factors = twiddle_ref[pl.ds(row, step), :]
        for x in range(RADIX):
            value = z[x]
            if x:
                cos = jnp.broadcast_to(factors[:, x : x + 1], (step, LANES))
                sin = jnp.broadcast_to(factors[:, RADIX + x : RADIX + x + 1], (step, LANES))
                value = ops.mul(value, cos, sin)
            real[where[x], :] = value[0]
            imag[where[x], :] = jnp.zeros((step, LANES), jnp.float32) if value[1] is None else value[1]
        return carry

    lax.fori_loop(0, DENSE // step, butterflies, 0)

    def products(x, carry):
        at = pl.ds(pl.multiple_of(x * DENSE, DENSE), DENSE)
        both = dense_product(table_ref, jnp.concatenate([real[at, :], imag[at, :]], axis=1))
        rows = pl.ds(x, DENSE, stride=RADIX)
        real_out[rows, :] = both[:DENSE, :LANES] - both[DENSE:, LANES:]
        imag_out[rows, :] = both[DENSE:, :LANES] + both[:DENSE, LANES:]
        return carry

    lax.fori_loop(0, RADIX, products, 0)
    for r in range(n_rows):
        for c in range(n_cols):
            for j in range(2):
                row = (c * n_rows + r) * LANES + j * HALF
                tile = jnp.concatenate([real_out[row : row + HALF, :], imag_out[row : row + HALF, :]], axis=0)
                outs[j][r * n_cols + c] = tile.T


def cell_kernel(n_cov, place, coefficients, latent_ref, cov_ref, counts_ref, mask_ref, residual_ref, sums_ref):
    @pl.when(pl.program_id(0) == 0)
    def _():
        sums_ref[...] = jnp.zeros_like(sums_ref)

    height = latent_ref.shape[0]
    width = latent_ref.shape[1]
    step = 16

    def fold(value):
        return value[:8] + value[8:]

    for row in range(0, height, step):
        rows = slice(row, row + step)

        def body(t, carry, rows=rows):
            lanes = pl.ds(pl.multiple_of(t * LANES, LANES), LANES)
            total = latent_ref[rows, lanes] * (1.0 / NG)
            for j in range(n_cov):
                total += coefficients[j] * cov_ref[j, rows, lanes].astype(jnp.float32)
            intensity = jnp.exp(total)
            land = mask_ref[rows, lanes].astype(jnp.float32)
            count = counts_ref[rows, lanes].astype(jnp.float32)
            residual = land * (intensity - count)
            residual_ref[rows, lanes] = residual
            for j in range(n_cov):
                sums_ref[j] += fold(cov_ref[j, rows, lanes].astype(jnp.float32) * residual)
            sums_ref[n_cov] += fold(land * (intensity - count * total))
            return carry

        lax.fori_loop(0, width // LANES, body, 0)


def final_kernel(count, place, hyper, real_ref, imag_ref, *refs):
    blocks, (step_real_ref, step_imag_ref) = refs[: 2 * count], refs[2 * count :]
    height = real_ref.shape[0]
    me, first_row, first_col = place[0], place[1], place[2]
    lane = lax.broadcasted_iota(jnp.int32, (1, LANES), 1)
    low = lane < HALF
    step = 64
    first_row = first_row + pl.program_id(0) * height
    for k in range(count):
        start = pl.multiple_of(jnp.bitwise_xor(me, k) * LANES, LANES)
        for row in range(0, height, step):
            rows = pl.ds(row, step)
            lanes = pl.ds(start, LANES)
            spec = spectrum_of(hyper, first_row + row, first_col + start, (step, LANES))
            inverse = 1.0 / (1.0 + spec * spec)
            spec = spec * (1.0 / NG)
            one, two = blocks[k][rows, :], blocks[count + k][rows, :]
            adjoint_real = jnp.where(low, one, pltpu.roll(two, HALF, 1))
            adjoint_imag = jnp.where(low, pltpu.roll(one, HALF, 1), two)
            step_real_ref[rows, lanes] = (spec * adjoint_real + real_ref[rows, lanes]) * inverse
            step_imag_ref[rows, lanes] = (imag_ref[rows, lanes] - spec * adjoint_imag) * inverse


SMEM = pl.BlockSpec(memory_space=pltpu.SMEM)
VMEM = pl.BlockSpec(memory_space=pltpu.VMEM)


def f32(*shape):
    return jax.ShapeDtypeStruct(shape, jnp.float32)


def params(mib):
    return pltpu.CompilerParams(vmem_limit_bytes=mib << 20)


def cost(flops, nbytes):
    return pl.CostEstimate(flops=int(flops), bytes_accessed=int(nbytes), transcendentals=0)


def call_scale(place, hyper, real, imag, n_rows):
    def kernel(*refs):
        scale_kernel(n_rows, *refs)

    height = real.shape[0]
    out = pl.pallas_call(
        kernel,
        name="scale",
        out_shape=[f32(height, LANES)] * (2 * n_rows) + [f32(8, LANES)],
        in_specs=[SMEM, SMEM, VMEM, VMEM],
        out_specs=[VMEM] * (2 * n_rows + 1),
        compiler_params=params(32),
        cost_estimate=cost(4e9, 4 * 4 * real.size),
    )(place, hyper, real, imag)
    return out[:n_rows], out[n_rows : 2 * n_rows], out[-1]


def call_first_axis(place, tables, ins, n_out):
    n_in = len(ins)

    def kernel(*refs):
        first_axis_kernel(n_in, n_out, *refs)

    return pl.pallas_call(
        kernel,
        name="first_axis",
        out_shape=[f32(NG // n_out, LANES)] * n_out,
        in_specs=[SMEM, VMEM, VMEM] + [VMEM] * n_in,
        out_specs=[VMEM] * n_out,
        scratch_shapes=[pltpu.VMEM((NG, LANES), jnp.float32)] * 2,
        compiler_params=params(32),
        cost_estimate=cost(5e9, 2 * 4 * NG * LANES),
    )(place, *tables, *ins)


def call_second_axis(place, tables, ins, n_rows, n_cols):
    def kernel(*refs):
        second_axis_kernel(n_rows, n_cols, *refs)

    return pl.pallas_call(
        kernel,
        name="second_axis",
        out_shape=[f32(LANES, NG // n_cols)] * n_cols,
        in_specs=[SMEM, VMEM, VMEM, VMEM, VMEM],
        out_specs=[VMEM] * n_cols,
        scratch_shapes=[pltpu.VMEM((NG, LANES), jnp.float32)] * 3,
        compiler_params=params(40),
        cost_estimate=cost(8e9, 3 * 4 * NG * LANES),
    )(place, *tables, *ins)


def call_second_axis_back(place, tables, ins, n_rows, n_cols):
    def kernel(*refs):
        second_axis_back_kernel(n_rows, n_cols, *refs)

    return pl.pallas_call(
        kernel,
        name="second_axis_back",
        out_shape=[f32(n_rows * n_cols, LANES, LANES)] * 2,
        in_specs=[SMEM, VMEM, VMEM] + [VMEM] * n_cols,
        out_specs=[VMEM] * 2,
        scratch_shapes=[pltpu.VMEM((NG, LANES), jnp.float32)] * 4,
        compiler_params=params(40),
        cost_estimate=cost(8e9, 3 * 4 * NG * LANES),
    )(place, *tables, *ins)


def call_cell(place, coefficients, latent, covariates, counts, mask, k):
    n_cov = covariates.shape[0]
    height, width = latent.shape
    tile = 32
    tiles = height // tile

    def kernel(*refs):
        cell_kernel(n_cov, *refs)

    def part(i, place, coefficients):
        return (jnp.bitwise_xor(place[3], k) * tiles + i, 0)

    return pl.pallas_call(
        kernel,
        name="cell",
        out_shape=[f32(height, width), f32(n_cov + 1, 8, LANES)],
        grid_spec=pltpu.PrefetchScalarGridSpec(
            num_scalar_prefetch=2,
            grid=(tiles,),
            in_specs=[
                pl.BlockSpec((tile, width), lambda i, p, c: (i, 0)),
                pl.BlockSpec((n_cov, tile, width), lambda i, p, c: (0, *part(i, p, c))),
                pl.BlockSpec((tile, width), part),
                pl.BlockSpec((tile, width), part),
            ],
            out_specs=[
                pl.BlockSpec((tile, width), lambda i, p, c: (i, 0)),
                pl.BlockSpec((n_cov + 1, 8, LANES), lambda i, p, c: (0, 0, 0)),
            ],
        ),
        compiler_params=params(32),
        cost_estimate=cost(4e9, height * width * (2 * n_cov + 16)),
    )(place, coefficients, latent, covariates, counts, mask)


def call_final(place, hyper, real, imag, blocks, n_rows):
    height, width = real.shape
    tile = 128

    def kernel(*refs):
        final_kernel(n_rows, *refs)

    wide = pl.BlockSpec((tile, width), lambda i: (i, 0))
    narrow = pl.BlockSpec((tile, LANES), lambda i: (i, 0))
    return pl.pallas_call(
        kernel,
        name="final",
        out_shape=[f32(height, width)] * 2,
        grid=(height // tile,),
        in_specs=[SMEM, SMEM, wide, wide] + [narrow] * (2 * n_rows),
        out_specs=[wide, wide],
        compiler_params=params(32),
        cost_estimate=cost(4e9, 6 * 4 * real.size),
    )(place, hyper, real, imag, *blocks)


def exchange(blocks, axis):
    count = len(blocks)
    received = [blocks[0]] + [None] * (count - 1)
    for k in range(count - 1, 0, -1):
        received[k] = lax.ppermute(blocks[k], axis, [(i, i ^ k) for i in range(count)])
    return received


def sum_over(values, mesh_axes):
    for axis, count in mesh_axes:
        k = 1
        while k < count:
            values = values + lax.ppermute(values, axis, [(i, i ^ k) for i in range(count)])
            k *= 2
    return values


def tiled_shards(n_rows, n_cols):
    def run(white_real, white_imag, covariates, coefficients, counts, land_mask, field_hyper):
        height, width = white_real.shape
        n_cov = covariates.shape[0]
        my_row, my_col = lax.axis_index("rows"), lax.axis_index("cols")
        place = jnp.stack([my_row, my_row * height, my_col * width, my_col]).astype(jnp.int32)
        spots = jnp.stack([my_row, my_col]).astype(jnp.int32)
        tables = (jnp.asarray(dense_table()), jnp.asarray(twiddle_table()))

        *packed, squares = call_scale(place, field_hyper, white_real, white_imag, n_rows)
        lines = []
        for j in range(2):
            columns = exchange(packed[j], "rows")
            (spread,) = call_first_axis(spots, tables, columns, 1)
            spread = spread.reshape(n_rows * n_cols, LANES, LANES)
            lines.append(lax.all_to_all(spread, ("rows", "cols"), 0, 0))
        latent = exchange(call_second_axis(spots, tables, lines, n_rows, n_cols), "cols")

        residuals, sums = [], 0.0
        for k in range(n_cols):
            residual, part = call_cell(place, coefficients, latent[k], covariates, counts, land_mask, k)
            residuals.append(residual)
            sums = sums + part
        back = exchange(residuals, "cols")
        spread = call_second_axis_back(spots, tables, back, n_rows, n_cols)
        blocks = []
        for j in range(2):
            lines = lax.all_to_all(spread[j], ("rows", "cols"), 0, 0).reshape(NG, LANES)
            blocks += exchange(call_first_axis(spots, tables, [lines], n_rows), "rows")

        sums = jnp.sum(sums, axis=(1, 2))
        own_loss = sums[n_cov] + 0.5 * jnp.sum(squares)
        own = jnp.concatenate([sums[:n_cov], jnp.broadcast_to(own_loss, (LANES - n_cov,))])
        totals = sum_over(own, (("rows", n_rows), ("cols", n_cols)))
        per_cell = 1.0 / (NG * NG)
        coef_grad = (
            totals[:n_cov] * per_cell + lasso_weight * jnp.sign(coefficients) + ridge_weight * coefficients
        )
        objective = (
            totals[n_cov] * per_cell
            + lasso_weight * jnp.sum(jnp.abs(coefficients))
            + 0.5 * ridge_weight * jnp.sum(coefficients * coefficients)
        )
        step_real, step_imag = call_final(place, field_hyper, white_real, white_imag, blocks, n_rows)
        return (step_real, step_imag, coef_grad, objective)

    return run


def field_spectrum(field_hyper, wave_row, wave_col):
    amplitude = 0.2 * field_hyper[0]
    freq_range = field_hyper[1]
    radius = (wave_row[:, None] * wave_row[:, None] + wave_col[None, :] * wave_col[None, :]) / (
        freq_range * freq_range
    )
    return amplitude * (1.0 + NG / freq_range * jnp.power(1.0 + radius, -0.75))


def angle_table(left_len, right_len, modulus):
    product = lax.iota(jnp.int32, left_len)[:, None] * lax.iota(jnp.int32, right_len)[None, :]
    angles = (product % modulus).astype(jnp.float32) * (2.0 * math.pi / modulus)
    return (jnp.cos(angles), jnp.sin(angles))


def inverse_transform(pieces, want_real):
    highest = lax.Precision.HIGHEST
    components = pieces.shape[0]
    row_count = pieces.shape[1]
    length = pieces.shape[2]
    factor = 8
    others = length // factor
    shaped = pieces.reshape(components, row_count, others, factor)
    big_cos, big_sin = angle_table(others, others, others)

    def apply_big(table, block):
        return jnp.einsum("rnm,nk->rmk", block, table, precision=highest)

    if components == 2:
        real_mid = apply_big(big_cos, shaped[0]) - apply_big(big_sin, shaped[1])
        imag_mid = apply_big(big_sin, shaped[0]) + apply_big(big_cos, shaped[1])
    else:
        real_mid = apply_big(big_cos, shaped[0])
        imag_mid = apply_big(big_sin, shaped[0])
    tw_cos, tw_sin = angle_table(factor, others, length)
    real_tw = real_mid * tw_cos - imag_mid * tw_sin
    imag_tw = real_mid * tw_sin + imag_mid * tw_cos
    small_cos, small_sin = angle_table(factor, factor, factor)

    def apply_small(table, block):
        return jnp.einsum("rmk,mj->rjk", block, table, precision=highest)

    real_out = (apply_small(small_cos, real_tw) - apply_small(small_sin, imag_tw)).reshape(
        1, row_count, length
    )
    if want_real:
        return real_out
    imag_out = (apply_small(small_sin, real_tw) + apply_small(small_cos, imag_tw)).reshape(
        1, row_count, length
    )
    return jnp.concatenate([real_out, imag_out], axis=0)


def middle_step(spread):
    returned = lax.all_to_all(spread, "cols", split_axis=2, concat_axis=1, tiled=True)
    flipped = jnp.swapaxes(returned, 1, 2)
    return lax.all_to_all(flipped, "rows", split_axis=1, concat_axis=2, tiled=True)


def grid_transform(pieces, want_real):
    full_rows = lax.all_to_all(pieces, "cols", split_axis=1, concat_axis=2, tiled=True)
    halfway = inverse_transform(full_rows, False)
    columns = middle_step(halfway)
    second = inverse_transform(columns, want_real)
    blocks_out = lax.all_to_all(second, "rows", split_axis=2, concat_axis=1, tiled=True)
    return jnp.swapaxes(blocks_out, 1, 2) * (1.0 / NG)


def shards(white_real, white_imag, covariates, coefficients, counts, land_mask, field_hyper):
    highest = lax.Precision.HIGHEST
    rows_here = white_real.shape[0]
    cols_here = white_real.shape[1]
    freq_row = lax.axis_index("rows") * rows_here + lax.iota(jnp.int32, rows_here)
    freq_col = lax.axis_index("cols") * cols_here + lax.iota(jnp.int32, cols_here)
    wave_row = jnp.minimum(freq_row, NG - freq_row).astype(jnp.float32)
    wave_col = jnp.minimum(freq_col, NG - freq_col).astype(jnp.float32)
    spectrum = field_spectrum(field_hyper, wave_row, wave_col)
    scaled = jnp.stack([spectrum * white_real, spectrum * white_imag])
    latent = grid_transform(scaled, True)[0]
    cov_full = covariates.astype(jnp.float32)
    linear = jnp.einsum("j,jrc->rc", coefficients, cov_full, precision=highest)
    log_rate = linear + latent
    intensity = jnp.exp(log_rate)
    land_vals = land_mask.astype(jnp.float32)
    count_vals = counts.astype(jnp.float32)
    residual = land_vals * (intensity - count_vals)
    partial_coef = jnp.einsum("jrc,rc->j", cov_full, residual, precision=highest)
    partial_loss = jnp.sum(land_vals * (intensity - count_vals * log_rate)) + 0.5 * jnp.sum(
        white_real * white_real + white_imag * white_imag
    )
    adjoint = grid_transform(residual[None], False)
    total_coef, total_loss = lax.psum((partial_coef, partial_loss), ("rows", "cols"))
    per_cell = 1.0 / (NG * NG)
    coef_grad = (
        total_coef * per_cell + lasso_weight * jnp.sign(coefficients) + ridge_weight * coefficients
    )
    objective = (
        total_loss * per_cell
        + lasso_weight * jnp.sum(jnp.abs(coefficients))
        + 0.5 * ridge_weight * jnp.sum(coefficients * coefficients)
    )
    curvature = 1.0 + spectrum * spectrum
    step_real = (spectrum * adjoint[0] + white_real) / curvature
    step_imag = (white_imag - spectrum * adjoint[1]) / curvature
    return (step_real, step_imag, coef_grad, objective)


def solution(mesh):
    n_rows, n_cols = mesh.shape["rows"], mesh.shape["cols"]
    tiled = n_rows * n_cols * LANES == NG and not n_rows & (n_rows - 1) and not n_cols & (n_cols - 1)
    return jax.shard_map(
        tiled_shards(n_rows, n_cols) if tiled else shards,
        mesh=mesh,
        in_specs=(
            P("rows", "cols"),
            P("rows", "cols"),
            P(None, "rows", "cols"),
            P(),
            P("rows", "cols"),
            P("rows", "cols"),
            P(),
        ),
        out_specs=(P("rows", "cols"), P("rows", "cols"), P(), P()),
        check_vma=False,
    )
```

```python
import math

import jax
import jax.numpy as jnp
import ml_dtypes
import numpy as np
from jax import lax
from jax.experimental import pallas as pl
from jax.experimental.pallas import tpu as pltpu
from jax.sharding import PartitionSpec as P

NG = 4096
LANES = 128
HALF = LANES // 2
RADIX = 16
DENSE = NG // RADIX

lasso_weight = 0.02
ridge_weight = 0.1


def split3(values):
    first = values.astype(ml_dtypes.bfloat16)
    rest = values - first.astype(np.float64)
    second = rest.astype(ml_dtypes.bfloat16)
    rest = rest - second.astype(np.float64)
    return first, second, rest.astype(ml_dtypes.bfloat16)


def dense_table():
    index = np.arange(DENSE)
    angles = (index[:, None] * index[None, :] % DENSE) * (2.0 * np.pi / DENSE)
    quarters = index.reshape(4, DENSE // 4)
    columns = [np.concatenate([quarters[j], quarters[j + 2]]) for j in range(2)]
    full = np.concatenate([part[:, at] for at in columns for part in (np.cos(angles), -np.sin(angles))], axis=1)
    return np.concatenate(split3(full), axis=1)


def twiddle_table():
    angles = np.arange(DENSE)[None, :] * np.array([1.0, 4.0])[:, None] * (2.0 * np.pi / NG)
    return np.stack([np.cos(angles[0]), np.sin(angles[0]), np.cos(angles[1]), np.sin(angles[1])]).astype(np.float32)


class Pairs:
    def add(self, a, b):
        return tuple(y if x is None else x if y is None else x + y for x, y in zip(a, b))

    def sub(self, a, b):
        return tuple((None if y is None else -y) if x is None else x if y is None else x - y for x, y in zip(a, b))

    def turn(self, a):
        return (None if a[1] is None else -a[1], a[0])

    def mul(self, a, c, s):
        re, im = a
        if im is None:
            return (re * c, re * s)
        if re is None:
            return (-(im * s), im * c)
        return (re * c - im * s, re * s + im * c)


def dft4(ops, z):
    even, odd = ops.add(z[0], z[2]), ops.sub(z[0], z[2])
    even2, turned = ops.add(z[1], z[3]), ops.turn(ops.sub(z[1], z[3]))
    return [ops.add(even, even2), ops.add(odd, turned), ops.sub(even, even2), ops.sub(odd, turned)]


def dft16(ops, z):
    columns = []
    for q in range(4):
        column = dft4(ops, [z[4 * p + q] for p in range(4)])
        for u in range(1, 4):
            turns = q * u
            if turns == 4:
                column[u] = ops.turn(column[u])
            elif turns:
                angle = 2.0 * math.pi * turns / RADIX
                column[u] = ops.mul(column[u], math.cos(angle), math.sin(angle))
        columns.append(column)
    out = [None] * RADIX
    for u in range(4):
        for v, value in enumerate(dft4(ops, [columns[q][u] for q in range(4)])):
            out[u + 4 * v] = value
    return out


def bf16_parts(values):
    one = values.astype(jnp.bfloat16)
    rest = values - one.astype(jnp.float32)
    two = rest.astype(jnp.bfloat16)
    return [one, two, (rest - two.astype(jnp.float32)).astype(jnp.bfloat16)]


def dense_product(table, first, parts):
    one, two, three = parts
    depth = one.shape[0]

    def dot(part, right):
        start = 2 * DENSE * part + first
        return jnp.dot(table[:, start : start + depth], right, preferred_element_type=jnp.float32)

    small = (dot(2, one) + dot(0, three)) + dot(1, two)
    return (small + (dot(1, one) + dot(0, two))) + dot(0, one)


def powers(twiddle_ref, row, step):
    ops = Pairs()
    w = [None] * RADIX
    at = pl.ds(row, step)
    w[1] = (twiddle_ref[0, at, :], twiddle_ref[1, at, :])
    w[4] = (twiddle_ref[2, at, :], twiddle_ref[3, at, :])
    w[2] = ops.mul(w[1], *w[1])
    w[3] = ops.mul(w[2], *w[1])
    for x in (5, 6, 7):
        w[x] = ops.mul(w[4], *w[x - 4])
    w[8] = ops.mul(w[4], *w[4])
    for x in range(9, RADIX):
        w[x] = ops.mul(w[8], *w[x - 8])
    return w


def butterflies(load, re_ref, im_ref, twiddle_ref, halves=(0, 1)):
    ops = Pairs()
    step = 8
    quarter = DENSE // 4
    for at, j in enumerate(halves):

        def body(i, carry, at=at, j=j):
            slow = i // (quarter // step)
            inner = pl.multiple_of((i % (quarter // step)) * step, step)
            z = dft16(ops, [load(a, 2 * slow + j, inner) for a in range(RADIX)])
            w = powers(twiddle_ref, pl.multiple_of((2 * slow + j) * quarter + inner, step), step)
            for x in range(RADIX):
                re, im = ops.mul(z[x], *w[x]) if x else z[x]
                rows = pl.ds(pl.multiple_of((x * len(halves) + at) * 2 * quarter + i * step, step), step)
                re_ref[rows, :] = re
                im_ref[rows, :] = jnp.zeros((step, LANES), jnp.float32) if im is None else im
            return carry

        lax.fori_loop(0, 2 * quarter // step, body, 0, unroll=4)


def stacked(re_ref, im_ref, x, n_halves):
    half = DENSE // 2
    out = []
    for h in range(n_halves):
        rows = pl.ds(pl.multiple_of((x * n_halves + h) * half, half), half)
        out += [re_ref[rows, :], im_ref[rows, :]]
    return out


def real_products(re_ref, im_ref, table_ref, target, halves=(0, 1)):
    def body(p, carry):
        pair = [jnp.concatenate(stacked(re_ref, im_ref, 2 * p + h, len(halves)), axis=0) for h in range(2)]
        both = dense_product(table_ref, halves[0] * DENSE, bf16_parts(jnp.concatenate(pair, axis=1)))
        for h in range(2):
            target[pl.ds(2 * p + h, DENSE, stride=RADIX), :] = both[:, h * LANES : (h + 1) * LANES]
        return carry

    lax.fori_loop(0, RADIX // 2, body, 0, unroll=4)


def spectrum_of(hyper, first_row, first_col, shape, cols=None):
    rows = lax.broadcasted_iota(jnp.int32, shape, 0) + first_row
    cols = (lax.broadcasted_iota(jnp.int32, shape, 1) if cols is None else cols) + first_col
    wave_row = jnp.minimum(rows, NG - rows).astype(jnp.float32)
    wave_col = jnp.minimum(cols, NG - cols).astype(jnp.float32)
    amplitude = 0.2 * hyper[0]
    span = hyper[1]
    base = 1.0 + (wave_row * wave_row + wave_col * wave_col) * (1.0 / (span * span))
    return amplitude * (1.0 + (NG / span) / jnp.sqrt(base * jnp.sqrt(base)))


def scale_kernel(count, j, place, hyper, real_ref, imag_ref, *outs):
    height = real_ref.shape[0]
    me, first_col = place[0], place[2]
    first_row = place[1] + pl.program_id(0) * height
    lane = lax.broadcasted_iota(jnp.int32, (1, LANES), 1)
    low = lane < HALF
    step = 64
    total = jnp.zeros((8, LANES), jnp.float32)
    for k in range(count):
        start = pl.multiple_of(jnp.bitwise_xor(me, k) * LANES, LANES)
        for row in range(0, height, step):
            real = real_ref[pl.ds(row, step), pl.ds(start, LANES)]
            imag = imag_ref[pl.ds(row, step), pl.ds(start, LANES)]
            squares = real * real + imag * imag
            squares = jnp.where(low, squares, 0.0) if j == 0 else jnp.where(low, 0.0, squares)
            total += jnp.sum(squares.reshape(step // 8, 8, LANES), axis=0)
            if j == 0:
                value = jnp.where(low, real, pltpu.roll(imag, HALF, 1))
            else:
                value = jnp.where(low, pltpu.roll(real, HALF, 1), imag)
            cols = jnp.bitwise_and(lax.broadcasted_iota(jnp.int32, (step, LANES), 1), HALF - 1)
            spec = spectrum_of(hyper, first_row + row, first_col + start + j * HALF, (step, LANES), cols)
            outs[k][pl.ds(row, step), :] = spec * value
    outs[-1][...] = total


def first_axis_kernel(n_in, n_out, place, table_ref, twiddle_ref, *refs):
    ins, outs, (one, two, done) = refs[:n_in], refs[n_in : n_in + n_out], refs[n_in + n_out :]
    me = place[0]
    lane = lax.broadcasted_iota(jnp.int32, (8, LANES), 1)
    sign = jnp.where(lane < HALF, 1.0, -1.0).astype(jnp.float32)
    if n_in > 1:
        height = ins[0].shape[0]
        for k in range(n_in):
            start = pl.multiple_of(jnp.bitwise_xor(me, k) * height, height)
            done[pl.ds(start, height), :] = ins[k][...]
        source = done
    else:
        source = ins[0]
    target = done if n_out > 1 else outs[0]

    def load(a, quarter, inner):
        row = pl.multiple_of(a * DENSE + quarter * (DENSE // 4) + inner, 8)
        value = source[pl.ds(row, 8), :]
        return (value, pltpu.roll(value, HALF, 1) * sign)

    butterflies(load, one, two, twiddle_ref)
    real_products(one, two, table_ref, target)
    if n_out > 1:
        height = outs[0].shape[0]
        for k in range(n_out):
            start = pl.multiple_of(jnp.bitwise_xor(me, k) * height, height)
            outs[k][...] = done[pl.ds(start, height), :]


def second_axis_kernel(n_rows, n_cols, j, place, table_ref, twiddle_ref, *refs):
    lines, refs = refs[0], refs[1:]
    last = j == 1
    if last:
        before, outs, (real, imag, done) = refs[0], refs[1 : 1 + n_cols], refs[1 + n_cols :]
    else:
        done, real, imag = refs
    me = place[1]
    for r in range(n_rows):
        for c in range(n_cols):
            turned = lines[r * n_cols + c].T
            row = (c * n_rows + r) * HALF
            real[row : row + HALF, :] = turned[:HALF]
            imag[row : row + HALF, :] = turned[HALF:]

    def load(a, quarter, inner):
        rows = pl.ds(pl.multiple_of(2 * a * HALF + (quarter // 2) * HALF + inner, 8), 8)
        return (real[rows, :], imag[rows, :])

    butterflies(load, real, imag, twiddle_ref, (j,))
    real_products(real, imag, table_ref, done, (j,))
    if not last:
        return
    width = NG // n_cols
    for k in range(n_cols):
        start = jnp.bitwise_xor(me, k) * width
        rows = pl.ds(pl.multiple_of(start, LANES), width)
        outs[k][...] = done[rows, :] + before[rows, :]


def second_axis_back_kernel(n_rows, n_cols, place, table_ref, twiddle_ref, *refs):
    ins, outs, (real, imag, real_out, imag_out) = refs[:n_cols], refs[n_cols : n_cols + 2], refs[n_cols + 2 :]
    source = real_out
    me = place[1]
    width = NG // n_cols
    for k in range(n_cols):
        start = jnp.bitwise_xor(me, k) * width
        source[pl.ds(pl.multiple_of(start, LANES), width), :] = ins[k][...]

    def load(a, quarter, inner):
        return (source[pl.ds(pl.multiple_of(a * DENSE + quarter * (DENSE // 4) + inner, 8), 8), :], None)

    butterflies(load, real, imag, twiddle_ref)

    def products(x, carry):
        pieces = [bf16_parts(piece) for piece in stacked(real, imag, x, 2)]
        parts = []
        for re0, im0, re1, im1 in zip(*pieces):
            left = jnp.concatenate([re0, im0, re1, im1], axis=0)
            right = jnp.concatenate([im0, -re0, im1, -re1], axis=0)
            parts.append(jnp.concatenate([left, right], axis=1))
        both = dense_product(table_ref, 0, parts)
        rows = pl.ds(x, DENSE, stride=RADIX)
        real_out[rows, :] = both[:, :LANES]
        imag_out[rows, :] = both[:, LANES:]
        return carry

    lax.fori_loop(0, RADIX, products, 0, unroll=4)
    for r in range(n_rows):
        for c in range(n_cols):
            for j in range(2):
                row = (c * n_rows + r) * LANES + j * HALF
                tile = jnp.concatenate([real_out[row : row + HALF, :], imag_out[row : row + HALF, :]], axis=0)
                outs[j][r * n_cols + c] = tile.T


def cell_kernel(n_cov, place, coefficients, latent_ref, cov_ref, counts_ref, mask_ref, residual_ref, sums_ref, values):
    @pl.when(pl.program_id(0) == 0)
    def _():
        sums_ref[...] = jnp.zeros_like(sums_ref)

    width = latent_ref.shape[0]
    step = 16
    for t in range(0, width, LANES):
        values[:, t : t + LANES] = latent_ref[t : t + LANES, :].T

    def fold(value):
        return value[:8] + value[8:]

    for row in range(0, LANES, step):
        rows = slice(row, row + step)

        def body(t, carry, rows=rows):
            lanes = pl.ds(pl.multiple_of(t * LANES, LANES), LANES)
            total = values[rows, lanes] * (1.0 / NG)
            for j in range(n_cov):
                total += coefficients[j] * cov_ref[j, rows, lanes].astype(jnp.float32)
            intensity = jnp.exp(total)
            land = mask_ref[rows, lanes].astype(jnp.float32)
            count = counts_ref[rows, lanes].astype(jnp.float32)
            residual = land * (intensity - count)
            values[rows, lanes] = residual
            for j in range(n_cov):
                sums_ref[j] += fold(cov_ref[j, rows, lanes].astype(jnp.float32) * residual)
            sums_ref[n_cov] += fold(land * (intensity - count * total))
            return carry

        lax.fori_loop(0, width // LANES, body, 0)
    for t in range(0, width, LANES):
        residual_ref[t : t + LANES, :] = values[:, t : t + LANES].T


def final_kernel(count, place, hyper, real_ref, imag_ref, *refs):
    blocks, (step_real_ref, step_imag_ref) = refs[: 2 * count], refs[2 * count :]
    height = real_ref.shape[0]
    me, first_row, first_col = place[0], place[1], place[2]
    lane = lax.broadcasted_iota(jnp.int32, (1, LANES), 1)
    low = lane < HALF
    step = 64
    first_row = first_row + pl.program_id(0) * height
    for k in range(count):
        start = pl.multiple_of(jnp.bitwise_xor(me, k) * LANES, LANES)
        for row in range(0, height, step):
            rows = pl.ds(row, step)
            lanes = pl.ds(start, LANES)
            spec = spectrum_of(hyper, first_row + row, first_col + start, (step, LANES))
            inverse = 1.0 / (1.0 + spec * spec)
            spec = spec * (1.0 / NG)
            one, two = blocks[k][rows, :], blocks[count + k][rows, :]
            adjoint_real = jnp.where(low, one, pltpu.roll(two, HALF, 1))
            adjoint_imag = jnp.where(low, pltpu.roll(one, HALF, 1), two)
            step_real_ref[rows, lanes] = (spec * adjoint_real + real_ref[rows, lanes]) * inverse
            step_imag_ref[rows, lanes] = (imag_ref[rows, lanes] - spec * adjoint_imag) * inverse


SMEM = pl.BlockSpec(memory_space=pltpu.SMEM)
VMEM = pl.BlockSpec(memory_space=pltpu.VMEM)


def f32(*shape):
    return jax.ShapeDtypeStruct(shape, jnp.float32)


def params(mib):
    return pltpu.CompilerParams(vmem_limit_bytes=mib << 20)


def cost(flops, nbytes):
    return pl.CostEstimate(flops=int(flops), bytes_accessed=int(nbytes), transcendentals=0)


def call_scale(place, hyper, real, imag, n_rows, j):
    height, width = real.shape
    tile = 128

    def kernel(*refs):
        scale_kernel(n_rows, j, *refs)

    wide = pl.BlockSpec((tile, width), lambda i: (i, 0))
    narrow = pl.BlockSpec((tile, LANES), lambda i: (i, 0))
    *out, squares = pl.pallas_call(
        kernel,
        name="scale",
        out_shape=[f32(height, LANES)] * n_rows + [f32(8 * height // tile, LANES)],
        grid=(height // tile,),
        in_specs=[SMEM, SMEM, wide, wide],
        out_specs=[narrow] * n_rows + [pl.BlockSpec((8, LANES), lambda i: (i, 0))],
        compiler_params=params(60),
        cost_estimate=cost(2e9, 3 * 4 * real.size),
    )(place, hyper, real, imag)
    return out, jnp.sum(squares)


def call_first_axis(place, tables, ins, n_out):
    n_in = len(ins)

    def kernel(*refs):
        first_axis_kernel(n_in, n_out, *refs)

    return pl.pallas_call(
        kernel,
        name="first_axis",
        out_shape=[f32(NG // n_out, LANES)] * n_out,
        in_specs=[SMEM, VMEM, VMEM] + [VMEM] * n_in,
        out_specs=[VMEM] * n_out,
        scratch_shapes=[pltpu.VMEM((NG, LANES), jnp.float32)] * 3,
        compiler_params=params(32),
        cost_estimate=cost(5e10, 2 * 4 * NG * LANES),
    )(place, *tables, *ins)


def call_second_axis(place, tables, lines, before, n_rows, n_cols):
    j = len(before)

    def kernel(*refs):
        second_axis_kernel(n_rows, n_cols, j, *refs)

    scratch = [pltpu.VMEM((NG // 2, LANES), jnp.float32)] * 2
    return pl.pallas_call(
        kernel,
        name="second_axis",
        out_shape=[f32(NG // n_cols, LANES)] * n_cols if j else f32(NG, LANES),
        in_specs=[SMEM, VMEM, VMEM, VMEM] + [VMEM] * j,
        out_specs=[VMEM] * n_cols if j else VMEM,
        scratch_shapes=scratch + [pltpu.VMEM((NG, LANES), jnp.float32)] * j,
        compiler_params=params(32),
        cost_estimate=cost(5e10, 3 * 4 * NG * LANES),
    )(place, *tables, lines, *before)


def call_second_axis_back(place, tables, ins, n_rows, n_cols):
    def kernel(*refs):
        second_axis_back_kernel(n_rows, n_cols, *refs)

    return pl.pallas_call(
        kernel,
        name="second_axis_back",
        out_shape=[f32(n_rows * n_cols, LANES, LANES)] * 2,
        in_specs=[SMEM, VMEM, VMEM] + [VMEM] * n_cols,
        out_specs=[VMEM] * 2,
        scratch_shapes=[pltpu.VMEM((NG, LANES), jnp.float32)] * 4,
        compiler_params=params(40),
        cost_estimate=cost(5e10, 3 * 4 * NG * LANES),
    )(place, *tables, *ins)


def call_cell(place, coefficients, latent, covariates, counts, mask, k):
    n_cov = covariates.shape[0]
    width = latent.shape[0]
    tile = 256

    def kernel(*refs):
        cell_kernel(n_cov, *refs)

    def part(i, place, coefficients):
        return (jnp.bitwise_xor(place[3], k), i)

    lines = pl.BlockSpec((tile, LANES), lambda i, p, c: (i, 0))
    return pl.pallas_call(
        kernel,
        name="cell",
        out_shape=[f32(width, LANES), f32(n_cov + 1, 8, LANES)],
        grid_spec=pltpu.PrefetchScalarGridSpec(
            num_scalar_prefetch=2,
            grid=(width // tile,),
            in_specs=[
                lines,
                pl.BlockSpec((n_cov, LANES, tile), lambda i, p, c: (0, *part(i, p, c))),
                pl.BlockSpec((LANES, tile), part),
                pl.BlockSpec((LANES, tile), part),
            ],
            out_specs=[lines, pl.BlockSpec((n_cov + 1, 8, LANES), lambda i, p, c: (0, 0, 0))],
            scratch_shapes=[pltpu.VMEM((LANES, tile), jnp.float32)],
        ),
        compiler_params=params(32),
        cost_estimate=cost(2e10, width * LANES * (2 * n_cov + 16)),
    )(place, coefficients, latent, covariates, counts, mask)


def call_final(place, hyper, real, imag, blocks, n_rows):
    height, width = real.shape
    tile = 128

    def kernel(*refs):
        final_kernel(n_rows, *refs)

    wide = pl.BlockSpec((tile, width), lambda i: (i, 0))
    narrow = pl.BlockSpec((tile, LANES), lambda i: (i, 0))
    return pl.pallas_call(
        kernel,
        name="final",
        out_shape=[f32(height, width)] * 2,
        grid=(height // tile,),
        in_specs=[SMEM, SMEM, wide, wide] + [narrow] * (2 * n_rows),
        out_specs=[wide, wide],
        compiler_params=params(60),
        cost_estimate=cost(4e9, 6 * 4 * real.size),
    )(place, hyper, real, imag, *blocks)


def exchange(blocks, axis):
    count = len(blocks)
    received = [blocks[0]] + [None] * (count - 1)
    for k in range(count - 1, 0, -1):
        received[k] = lax.ppermute(blocks[k], axis, [(i, i ^ k) for i in range(count)])
    return received


def doubled(values, axis, count, steps):
    for step in steps:
        values = values + lax.ppermute(values, axis, [(i, i ^ (1 << step)) for i in range(count)])
    return values


def tiled_shards(n_rows, n_cols):
    def run(white_real, white_imag, covariates, coefficients, counts, land_mask, field_hyper):
        height, width = white_real.shape
        n_cov = covariates.shape[0]
        my_row, my_col = lax.axis_index("rows"), lax.axis_index("cols")
        place = jnp.stack([my_row, my_row * height, my_col * width, my_col]).astype(jnp.int32)
        spots = jnp.stack([my_row, my_col]).astype(jnp.int32)
        twiddles = jnp.broadcast_to(jnp.asarray(twiddle_table())[:, :, None], (4, DENSE, LANES))
        tables = (jnp.asarray(dense_table()), twiddles)

        partial, squares = (), 0.0
        for j in range(2):
            scaled, part = call_scale(place, field_hyper, white_real, white_imag, n_rows, j)
            squares = squares + part
            if j:
                columns[1], *scaled = lax.optimization_barrier((columns[1], *scaled))
            columns = exchange(scaled, "rows")
            (spread,) = call_first_axis(spots, tables, columns, 1)
            spread = spread.reshape(n_rows * n_cols, LANES, LANES)
            lines = lax.all_to_all(spread, ("rows", "cols"), 0, 0)
            if j:
                latent = exchange(call_second_axis(spots, tables, lines, partial, n_rows, n_cols), "cols")
            else:
                partial = (call_second_axis(spots, tables, lines, partial, n_rows, n_cols),)

        residuals, sums = [], 0.0
        for k in range(n_cols):
            residual, part = call_cell(place, coefficients, latent[k], covariates, counts, land_mask, k)
            residuals.append(residual)
            sums = sums + part
        back = exchange(residuals, "cols")
        sums = jnp.sum(sums, axis=(1, 2))
        own_loss = sums[n_cov] + 0.5 * squares
        own = jnp.concatenate([sums[:n_cov], jnp.broadcast_to(own_loss, (LANES - n_cov,))])
        row_steps, col_steps = n_rows.bit_length() - 1, n_cols.bit_length() - 1
        totals = doubled(doubled(own, "rows", n_rows, range(row_steps)), "cols", n_cols, range(col_steps))
        spread = call_second_axis_back(spots, tables, back, n_rows, n_cols)
        blocks = []
        for j in range(2):
            lines = lax.all_to_all(spread[j], ("rows", "cols"), 0, 0).reshape(NG, LANES)
            if j:
                lines, *blocks = lax.optimization_barrier((lines, *blocks))
            else:
                lines, totals = lax.optimization_barrier((lines, totals))
            blocks += exchange(call_first_axis(spots, tables, [lines], n_rows), "rows")

        per_cell = 1.0 / (NG * NG)
        coef_grad = (
            totals[:n_cov] * per_cell + lasso_weight * jnp.sign(coefficients) + ridge_weight * coefficients
        )
        objective = (
            totals[n_cov] * per_cell
            + lasso_weight * jnp.sum(jnp.abs(coefficients))
            + 0.5 * ridge_weight * jnp.sum(coefficients * coefficients)
        )
        step_real, step_imag = call_final(place, field_hyper, white_real, white_imag, blocks, n_rows)
        return (step_real, step_imag, coef_grad, objective)

    return run


def field_spectrum(field_hyper, wave_row, wave_col):
    amplitude = 0.2 * field_hyper[0]
    freq_range = field_hyper[1]
    radius = (wave_row[:, None] * wave_row[:, None] + wave_col[None, :] * wave_col[None, :]) / (
        freq_range * freq_range
    )
    return amplitude * (1.0 + NG / freq_range * jnp.power(1.0 + radius, -0.75))


def angle_table(left_len, right_len, modulus):
    product = lax.iota(jnp.int32, left_len)[:, None] * lax.iota(jnp.int32, right_len)[None, :]
    angles = (product % modulus).astype(jnp.float32) * (2.0 * math.pi / modulus)
    return (jnp.cos(angles), jnp.sin(angles))


def inverse_transform(pieces, want_real):
    highest = lax.Precision.HIGHEST
    components = pieces.shape[0]
    row_count = pieces.shape[1]
    length = pieces.shape[2]
    factor = 8
    others = length // factor
    shaped = pieces.reshape(components, row_count, others, factor)
    big_cos, big_sin = angle_table(others, others, others)

    def apply_big(table, block):
        return jnp.einsum("rnm,nk->rmk", block, table, precision=highest)

    if components == 2:
        real_mid = apply_big(big_cos, shaped[0]) - apply_big(big_sin, shaped[1])
        imag_mid = apply_big(big_sin, shaped[0]) + apply_big(big_cos, shaped[1])
    else:
        real_mid = apply_big(big_cos, shaped[0])
        imag_mid = apply_big(big_sin, shaped[0])
    tw_cos, tw_sin = angle_table(factor, others, length)
    real_tw = real_mid * tw_cos - imag_mid * tw_sin
    imag_tw = real_mid * tw_sin + imag_mid * tw_cos
    small_cos, small_sin = angle_table(factor, factor, factor)

    def apply_small(table, block):
        return jnp.einsum("rmk,mj->rjk", block, table, precision=highest)

    real_out = (apply_small(small_cos, real_tw) - apply_small(small_sin, imag_tw)).reshape(
        1, row_count, length
    )
    if want_real:
        return real_out
    imag_out = (apply_small(small_sin, real_tw) + apply_small(small_cos, imag_tw)).reshape(
        1, row_count, length
    )
    return jnp.concatenate([real_out, imag_out], axis=0)


def middle_step(spread):
    returned = lax.all_to_all(spread, "cols", split_axis=2, concat_axis=1, tiled=True)
    flipped = jnp.swapaxes(returned, 1, 2)
    return lax.all_to_all(flipped, "rows", split_axis=1, concat_axis=2, tiled=True)


def grid_transform(pieces, want_real):
    full_rows = lax.all_to_all(pieces, "cols", split_axis=1, concat_axis=2, tiled=True)
    halfway = inverse_transform(full_rows, False)
    columns = middle_step(halfway)
    second = inverse_transform(columns, want_real)
    blocks_out = lax.all_to_all(second, "rows", split_axis=2, concat_axis=1, tiled=True)
    return jnp.swapaxes(blocks_out, 1, 2) * (1.0 / NG)


def shards(white_real, white_imag, covariates, coefficients, counts, land_mask, field_hyper):
    highest = lax.Precision.HIGHEST
    rows_here = white_real.shape[0]
    cols_here = white_real.shape[1]
    freq_row = lax.axis_index("rows") * rows_here + lax.iota(jnp.int32, rows_here)
    freq_col = lax.axis_index("cols") * cols_here + lax.iota(jnp.int32, cols_here)
    wave_row = jnp.minimum(freq_row, NG - freq_row).astype(jnp.float32)
    wave_col = jnp.minimum(freq_col, NG - freq_col).astype(jnp.float32)
    spectrum = field_spectrum(field_hyper, wave_row, wave_col)
    scaled = jnp.stack([spectrum * white_real, spectrum * white_imag])
    latent = grid_transform(scaled, True)[0]
    cov_full = covariates.astype(jnp.float32)
    linear = jnp.einsum("j,jrc->rc", coefficients, cov_full, precision=highest)
    log_rate = linear + latent
    intensity = jnp.exp(log_rate)
    land_vals = land_mask.astype(jnp.float32)
    count_vals = counts.astype(jnp.float32)
    residual = land_vals * (intensity - count_vals)
    partial_coef = jnp.einsum("jrc,rc->j", cov_full, residual, precision=highest)
    partial_loss = jnp.sum(land_vals * (intensity - count_vals * log_rate)) + 0.5 * jnp.sum(
        white_real * white_real + white_imag * white_imag
    )
    adjoint = grid_transform(residual[None], False)
    total_coef, total_loss = lax.psum((partial_coef, partial_loss), ("rows", "cols"))
    per_cell = 1.0 / (NG * NG)
    coef_grad = (
        total_coef * per_cell + lasso_weight * jnp.sign(coefficients) + ridge_weight * coefficients
    )
    objective = (
        total_loss * per_cell
        + lasso_weight * jnp.sum(jnp.abs(coefficients))
        + 0.5 * ridge_weight * jnp.sum(coefficients * coefficients)
    )
    curvature = 1.0 + spectrum * spectrum
    step_real = (spectrum * adjoint[0] + white_real) / curvature
    step_imag = (white_imag - spectrum * adjoint[1]) / curvature
    return (step_real, step_imag, coef_grad, objective)


def solution(mesh):
    n_rows, n_cols = mesh.shape["rows"], mesh.shape["cols"]
    tiled = n_rows * n_cols * LANES == NG and not n_rows & (n_rows - 1) and not n_cols & (n_cols - 1)
    return jax.shard_map(
        tiled_shards(n_rows, n_cols) if tiled else shards,
        mesh=mesh,
        in_specs=(
            P("rows", "cols"),
            P("rows", "cols"),
            P(None, "rows", "cols"),
            P(),
            P("rows", "cols"),
            P("rows", "cols"),
            P(),
        ),
        out_specs=(P("rows", "cols"), P("rows", "cols"), P(), P()),
        check_vma=False,
    )
```

```python
import math

import jax
import jax.numpy as jnp
import ml_dtypes
import numpy as np
from jax import lax
from jax.experimental import pallas as pl
from jax.experimental.pallas import tpu as pltpu
from jax.sharding import PartitionSpec as P

NG = 4096
LANES = 128
HALF = LANES // 2
RADIX = 16
DENSE = NG // RADIX

lasso_weight = 0.02
ridge_weight = 0.1


def split3(values):
    first = values.astype(ml_dtypes.bfloat16)
    rest = values - first.astype(np.float64)
    second = rest.astype(ml_dtypes.bfloat16)
    rest = rest - second.astype(np.float64)
    return first, second, rest.astype(ml_dtypes.bfloat16)


def dense_table():
    index = np.arange(DENSE)
    angles = (index[:, None] * index[None, :] % DENSE) * (2.0 * np.pi / DENSE)
    quarters = index.reshape(4, DENSE // 4)
    columns = [np.concatenate([quarters[j], quarters[j + 2]]) for j in range(2)]
    full = np.concatenate([part[:, at] for at in columns for part in (np.cos(angles), -np.sin(angles))], axis=1)
    return np.concatenate(split3(full), axis=1)


def twiddle_table():
    angles = np.arange(DENSE)[None, :] * np.array([1.0, 4.0])[:, None] * (2.0 * np.pi / NG)
    return np.stack([np.cos(angles[0]), np.sin(angles[0]), np.cos(angles[1]), np.sin(angles[1])]).astype(np.float32)


class Pairs:
    def add(self, a, b):
        return tuple(y if x is None else x if y is None else x + y for x, y in zip(a, b))

    def sub(self, a, b):
        return tuple((None if y is None else -y) if x is None else x if y is None else x - y for x, y in zip(a, b))

    def turn(self, a):
        return (None if a[1] is None else -a[1], a[0])

    def mul(self, a, c, s):
        re, im = a
        if im is None:
            return (re * c, re * s)
        if re is None:
            return (-(im * s), im * c)
        return (re * c - im * s, re * s + im * c)


def dft4(ops, z):
    even, odd = ops.add(z[0], z[2]), ops.sub(z[0], z[2])
    even2, turned = ops.add(z[1], z[3]), ops.turn(ops.sub(z[1], z[3]))
    return [ops.add(even, even2), ops.add(odd, turned), ops.sub(even, even2), ops.sub(odd, turned)]


def dft16(ops, z):
    columns = []
    for q in range(4):
        column = dft4(ops, [z[4 * p + q] for p in range(4)])
        for u in range(1, 4):
            turns = q * u
            if turns == 4:
                column[u] = ops.turn(column[u])
            elif turns:
                angle = 2.0 * math.pi * turns / RADIX
                column[u] = ops.mul(column[u], math.cos(angle), math.sin(angle))
        columns.append(column)
    out = [None] * RADIX
    for u in range(4):
        for v, value in enumerate(dft4(ops, [columns[q][u] for q in range(4)])):
            out[u + 4 * v] = value
    return out


def bf16_parts(values):
    one = values.astype(jnp.bfloat16)
    rest = values - one.astype(jnp.float32)
    two = rest.astype(jnp.bfloat16)
    return [one, two, (rest - two.astype(jnp.float32)).astype(jnp.bfloat16)]


def dense_product(table, first, parts):
    one, two, three = parts
    depth = one.shape[0]

    def dot(part, right):
        start = 2 * DENSE * part + first
        return jnp.dot(table[:, start : start + depth], right, preferred_element_type=jnp.float32)

    small = (dot(2, one) + dot(0, three)) + dot(1, two)
    return (small + (dot(1, one) + dot(0, two))) + dot(0, one)


def powers(twiddle_ref, row, step):
    ops = Pairs()
    w = [None] * RADIX
    at = pl.ds(row, step)
    w[1] = (twiddle_ref[0, at, :], twiddle_ref[1, at, :])
    w[4] = (twiddle_ref[2, at, :], twiddle_ref[3, at, :])
    w[2] = ops.mul(w[1], *w[1])
    w[3] = ops.mul(w[2], *w[1])
    for x in (5, 6, 7):
        w[x] = ops.mul(w[4], *w[x - 4])
    w[8] = ops.mul(w[4], *w[4])
    for x in range(9, RADIX):
        w[x] = ops.mul(w[8], *w[x - 8])
    return w


def butterflies(load, re_ref, im_ref, twiddle_ref, halves=(0, 1)):
    ops = Pairs()
    step = 8
    quarter = DENSE // 4
    for at, j in enumerate(halves):

        def body(i, carry, at=at, j=j):
            slow = i // (quarter // step)
            inner = pl.multiple_of((i % (quarter // step)) * step, step)
            z = dft16(ops, [load(a, 2 * slow + j, inner) for a in range(RADIX)])
            w = powers(twiddle_ref, pl.multiple_of((2 * slow + j) * quarter + inner, step), step)
            for x in range(RADIX):
                re, im = ops.mul(z[x], *w[x]) if x else z[x]
                rows = pl.ds(pl.multiple_of((x * len(halves) + at) * 2 * quarter + i * step, step), step)
                re_ref[rows, :] = re
                im_ref[rows, :] = jnp.zeros((step, LANES), jnp.float32) if im is None else im
            return carry

        lax.fori_loop(0, 2 * quarter // step, body, 0, unroll=4)


def stacked(re_ref, im_ref, x, n_halves):
    half = DENSE // 2
    out = []
    for h in range(n_halves):
        rows = pl.ds(pl.multiple_of((x * n_halves + h) * half, half), half)
        out += [re_ref[rows, :], im_ref[rows, :]]
    return out


def real_products(re_ref, im_ref, table_ref, target, halves=(0, 1)):
    def body(p, carry):
        pair = [jnp.concatenate(stacked(re_ref, im_ref, 2 * p + h, len(halves)), axis=0) for h in range(2)]
        both = dense_product(table_ref, halves[0] * DENSE, bf16_parts(jnp.concatenate(pair, axis=1)))
        for h in range(2):
            target[pl.ds(2 * p + h, DENSE, stride=RADIX), :] = both[:, h * LANES : (h + 1) * LANES]
        return carry

    lax.fori_loop(0, RADIX // 2, body, 0, unroll=4)


def spectrum_of(hyper, first_row, first_col, shape, cols=None):
    rows = lax.broadcasted_iota(jnp.int32, shape, 0) + first_row
    cols = (lax.broadcasted_iota(jnp.int32, shape, 1) if cols is None else cols) + first_col
    wave_row = jnp.minimum(rows, NG - rows).astype(jnp.float32)
    wave_col = jnp.minimum(cols, NG - cols).astype(jnp.float32)
    amplitude = 0.2 * hyper[0]
    span = hyper[1]
    root = lax.rsqrt(1.0 + (wave_row * wave_row + wave_col * wave_col) * (1.0 / (span * span)))
    return amplitude + (amplitude * (NG / span)) * (root * root * lax.rsqrt(root))


def scale_kernel(count, j, place, hyper, real_ref, imag_ref, *outs):
    height = real_ref.shape[0]
    me, first_col = place[0], place[2]
    first_row = place[1] + pl.program_id(0) * height
    lane = lax.broadcasted_iota(jnp.int32, (1, LANES), 1)
    low = lane < HALF
    step = 64
    total = jnp.zeros((8, LANES), jnp.float32)
    for k in range(count):
        start = pl.multiple_of(jnp.bitwise_xor(me, k) * LANES, LANES)
        for row in range(0, height, step):
            real = real_ref[pl.ds(row, step), pl.ds(start, LANES)]
            imag = imag_ref[pl.ds(row, step), pl.ds(start, LANES)]
            squares = real * real + imag * imag
            squares = jnp.where(low, squares, 0.0) if j == 0 else jnp.where(low, 0.0, squares)
            total += jnp.sum(squares.reshape(step // 8, 8, LANES), axis=0)
            if j == 0:
                value = jnp.where(low, real, pltpu.roll(imag, HALF, 1))
            else:
                value = jnp.where(low, pltpu.roll(real, HALF, 1), imag)
            cols = jnp.bitwise_and(lax.broadcasted_iota(jnp.int32, (step, LANES), 1), HALF - 1)
            spec = spectrum_of(hyper, first_row + row, first_col + start + j * HALF, (step, LANES), cols)
            outs[k][pl.ds(row, step), :] = spec * value
    outs[-1][...] = total


def first_axis_kernel(n_in, n_out, place, table_ref, twiddle_ref, *refs):
    ins, outs, (one, two, done) = refs[:n_in], refs[n_in : n_in + n_out], refs[n_in + n_out :]
    me = place[0]
    lane = lax.broadcasted_iota(jnp.int32, (8, LANES), 1)
    sign = jnp.where(lane < HALF, 1.0, -1.0).astype(jnp.float32)
    if n_in > 1:
        height = ins[0].shape[0]
        for k in range(n_in):
            start = pl.multiple_of(jnp.bitwise_xor(me, k) * height, height)
            done[pl.ds(start, height), :] = ins[k][...]
        source = done
    else:
        source = ins[0]
    target = done if n_out > 1 else outs[0]

    def load(a, quarter, inner):
        row = pl.multiple_of(a * DENSE + quarter * (DENSE // 4) + inner, 8)
        value = source[pl.ds(row, 8), :]
        return (value, pltpu.roll(value, HALF, 1) * sign)

    butterflies(load, one, two, twiddle_ref)
    real_products(one, two, table_ref, target)
    if n_out > 1:
        height = outs[0].shape[0]
        for k in range(n_out):
            start = pl.multiple_of(jnp.bitwise_xor(me, k) * height, height)
            outs[k][...] = done[pl.ds(start, height), :]


def second_axis_kernel(n_rows, n_cols, j, place, table_ref, twiddle_ref, *refs):
    lines, refs = refs[0], refs[1:]
    last = j == 1
    if last:
        outs, (real, imag, done, before, arrived) = refs[1 : 1 + n_cols], refs[1 + n_cols :]
        copy = pltpu.make_async_copy(refs[0], before, arrived)
        copy.start()
    else:
        done, real, imag = refs
    me = place[1]
    for r in range(n_rows):
        for c in range(n_cols):
            turned = lines[r * n_cols + c].T
            row = (c * n_rows + r) * HALF
            real[row : row + HALF, :] = turned[:HALF]
            imag[row : row + HALF, :] = turned[HALF:]

    def load(a, quarter, inner):
        rows = pl.ds(pl.multiple_of(2 * a * HALF + (quarter // 2) * HALF + inner, 8), 8)
        return (real[rows, :], imag[rows, :])

    butterflies(load, real, imag, twiddle_ref, (j,))
    real_products(real, imag, table_ref, done, (j,))
    if not last:
        return
    copy.wait()
    width = NG // n_cols
    for k in range(n_cols):
        start = jnp.bitwise_xor(me, k) * width
        rows = pl.ds(pl.multiple_of(start, LANES), width)
        outs[k][...] = done[rows, :] + before[rows, :]


def second_axis_back_kernel(n_rows, n_cols, place, table_ref, twiddle_ref, *refs):
    ins, outs, (real, imag, real_out, imag_out) = refs[:n_cols], refs[n_cols : n_cols + 2], refs[n_cols + 2 :]
    source = real_out
    me = place[1]
    width = NG // n_cols
    for k in range(n_cols):
        start = jnp.bitwise_xor(me, k) * width
        source[pl.ds(pl.multiple_of(start, LANES), width), :] = ins[k][...]

    def load(a, quarter, inner):
        return (source[pl.ds(pl.multiple_of(a * DENSE + quarter * (DENSE // 4) + inner, 8), 8), :], None)

    butterflies(load, real, imag, twiddle_ref)

    def products(x, carry):
        pieces = [bf16_parts(piece) for piece in stacked(real, imag, x, 2)]
        parts = []
        for re0, im0, re1, im1 in zip(*pieces):
            left = jnp.concatenate([re0, im0, re1, im1], axis=0)
            right = jnp.concatenate([im0, -re0, im1, -re1], axis=0)
            parts.append(jnp.concatenate([left, right], axis=1))
        both = dense_product(table_ref, 0, parts)
        rows = pl.ds(x, DENSE, stride=RADIX)
        real_out[rows, :] = both[:, :LANES]
        imag_out[rows, :] = both[:, LANES:]
        return carry

    lax.fori_loop(0, RADIX, products, 0, unroll=4)
    for r in range(n_rows):
        for c in range(n_cols):
            for j in range(2):
                row = (c * n_rows + r) * LANES + j * HALF
                tile = jnp.concatenate([real_out[row : row + HALF, :], imag_out[row : row + HALF, :]], axis=0)
                outs[j][r * n_cols + c] = tile.T


def cell_kernel(n_cov, place, coefficients, latent_ref, cov_ref, counts_ref, mask_ref, residual_ref, sums_ref, values):
    @pl.when(pl.program_id(0) == 0)
    def _():
        sums_ref[...] = jnp.zeros_like(sums_ref)

    width = latent_ref.shape[0]
    step = 16
    for t in range(0, width, LANES):
        values[:, t : t + LANES] = latent_ref[t : t + LANES, :].T

    def fold(value):
        return value[:8] + value[8:]

    for row in range(0, LANES, step):
        rows = slice(row, row + step)

        def body(t, carry, rows=rows):
            lanes = pl.ds(pl.multiple_of(t * LANES, LANES), LANES)
            total = values[rows, lanes] * (1.0 / NG)
            for j in range(n_cov):
                total += coefficients[j] * cov_ref[j, rows, lanes].astype(jnp.float32)
            intensity = jnp.exp(total)
            land = mask_ref[rows, lanes].astype(jnp.float32)
            count = counts_ref[rows, lanes].astype(jnp.float32)
            residual = land * (intensity - count)
            values[rows, lanes] = residual
            for j in range(n_cov):
                sums_ref[j] += fold(cov_ref[j, rows, lanes].astype(jnp.float32) * residual)
            sums_ref[n_cov] += fold(land * (intensity - count * total))
            return carry

        lax.fori_loop(0, width // LANES, body, 0)
    for t in range(0, width, LANES):
        residual_ref[t : t + LANES, :] = values[:, t : t + LANES].T


def final_kernel(count, place, hyper, real_ref, imag_ref, *refs):
    blocks, (step_real_ref, step_imag_ref) = refs[: 2 * count], refs[2 * count :]
    height = real_ref.shape[0]
    me, first_row, first_col = place[0], place[1], place[2]
    lane = lax.broadcasted_iota(jnp.int32, (1, LANES), 1)
    low = lane < HALF
    step = 64
    first_row = first_row + pl.program_id(0) * height
    for k in range(count):
        start = pl.multiple_of(jnp.bitwise_xor(me, k) * LANES, LANES)
        for row in range(0, height, step):
            rows = pl.ds(row, step)
            lanes = pl.ds(start, LANES)
            spec = spectrum_of(hyper, first_row + row, first_col + start, (step, LANES))
            inverse = 1.0 / (1.0 + spec * spec)
            spec = spec * (1.0 / NG)
            one, two = blocks[k][rows, :], blocks[count + k][rows, :]
            adjoint_real = jnp.where(low, one, pltpu.roll(two, HALF, 1))
            adjoint_imag = jnp.where(low, pltpu.roll(one, HALF, 1), two)
            step_real_ref[rows, lanes] = (spec * adjoint_real + real_ref[rows, lanes]) * inverse
            step_imag_ref[rows, lanes] = (imag_ref[rows, lanes] - spec * adjoint_imag) * inverse


SMEM = pl.BlockSpec(memory_space=pltpu.SMEM)
VMEM = pl.BlockSpec(memory_space=pltpu.VMEM)


def f32(*shape):
    return jax.ShapeDtypeStruct(shape, jnp.float32)


def params(mib):
    return pltpu.CompilerParams(vmem_limit_bytes=mib << 20)


def cost(flops, nbytes):
    return pl.CostEstimate(flops=int(flops), bytes_accessed=int(nbytes), transcendentals=0)


def call_scale(place, hyper, real, imag, n_rows, j):
    height, width = real.shape
    tile = 128

    def kernel(*refs):
        scale_kernel(n_rows, j, *refs)

    wide = pl.BlockSpec((tile, width), lambda i: (i, 0))
    narrow = pl.BlockSpec((tile, LANES), lambda i: (i, 0))
    *out, squares = pl.pallas_call(
        kernel,
        name="scale",
        out_shape=[f32(height, LANES)] * n_rows + [f32(8 * height // tile, LANES)],
        grid=(height // tile,),
        in_specs=[SMEM, SMEM, wide, wide],
        out_specs=[narrow] * n_rows + [pl.BlockSpec((8, LANES), lambda i: (i, 0))],
        compiler_params=params(60),
        cost_estimate=cost(2e9, 3 * 4 * real.size),
    )(place, hyper, real, imag)
    return out, jnp.sum(squares)


def call_first_axis(place, tables, ins, n_out):
    n_in = len(ins)

    def kernel(*refs):
        first_axis_kernel(n_in, n_out, *refs)

    return pl.pallas_call(
        kernel,
        name="first_axis",
        out_shape=[f32(NG // n_out, LANES)] * n_out,
        in_specs=[SMEM, VMEM, VMEM] + [VMEM] * n_in,
        out_specs=[VMEM] * n_out,
        scratch_shapes=[pltpu.VMEM((NG, LANES), jnp.float32)] * 3,
        compiler_params=params(32),
        cost_estimate=cost(5e10, 2 * 4 * NG * LANES),
    )(place, *tables, *ins)


def call_second_axis(place, tables, lines, before, n_rows, n_cols):
    j = len(before)

    def kernel(*refs):
        second_axis_kernel(n_rows, n_cols, j, *refs)

    scratch = [pltpu.VMEM((NG // 2, LANES), jnp.float32)] * 2
    return pl.pallas_call(
        kernel,
        name="second_axis",
        out_shape=[f32(NG // n_cols, LANES)] * n_cols if j else f32(NG, LANES),
        in_specs=[SMEM, VMEM, VMEM, VMEM] + [pl.BlockSpec(memory_space=pl.ANY)] * j,
        out_specs=[VMEM] * n_cols if j else VMEM,
        scratch_shapes=scratch + ([pltpu.VMEM((NG, LANES), jnp.float32)] * 2 + [pltpu.SemaphoreType.DMA]) * j,
        compiler_params=params(32),
        cost_estimate=cost(5e10, 3 * 4 * NG * LANES),
    )(place, *tables, lines, *before)


def call_second_axis_back(place, tables, ins, n_rows, n_cols):
    def kernel(*refs):
        second_axis_back_kernel(n_rows, n_cols, *refs)

    return pl.pallas_call(
        kernel,
        name="second_axis_back",
        out_shape=[f32(n_rows * n_cols, LANES, LANES)] * 2,
        in_specs=[SMEM, VMEM, VMEM] + [VMEM] * n_cols,
        out_specs=[VMEM] * 2,
        scratch_shapes=[pltpu.VMEM((NG, LANES), jnp.float32)] * 4,
        compiler_params=params(40),
        cost_estimate=cost(5e10, 3 * 4 * NG * LANES),
    )(place, *tables, *ins)


def call_cell(place, coefficients, latent, covariates, counts, mask, k):
    n_cov = covariates.shape[0]
    width = latent.shape[0]
    tile = 256

    def kernel(*refs):
        cell_kernel(n_cov, *refs)

    def part(i, place, coefficients):
        return (jnp.bitwise_xor(place[3], k), i)

    lines = pl.BlockSpec((tile, LANES), lambda i, p, c: (i, 0))
    return pl.pallas_call(
        kernel,
        name="cell",
        out_shape=[f32(width, LANES), f32(n_cov + 1, 8, LANES)],
        grid_spec=pltpu.PrefetchScalarGridSpec(
            num_scalar_prefetch=2,
            grid=(width // tile,),
            in_specs=[
                lines,
                pl.BlockSpec((n_cov, LANES, tile), lambda i, p, c: (0, *part(i, p, c))),
                pl.BlockSpec((LANES, tile), part),
                pl.BlockSpec((LANES, tile), part),
            ],
            out_specs=[lines, pl.BlockSpec((n_cov + 1, 8, LANES), lambda i, p, c: (0, 0, 0))],
            scratch_shapes=[pltpu.VMEM((LANES, tile), jnp.float32)],
        ),
        compiler_params=params(32),
        cost_estimate=cost(2e10, width * LANES * (2 * n_cov + 16)),
    )(place, coefficients, latent, covariates, counts, mask)


def call_final(place, hyper, real, imag, blocks, n_rows):
    height, width = real.shape
    tile = 128

    def kernel(*refs):
        final_kernel(n_rows, *refs)

    wide = pl.BlockSpec((tile, width), lambda i: (i, 0))
    narrow = pl.BlockSpec((tile, LANES), lambda i: (i, 0))
    return pl.pallas_call(
        kernel,
        name="final",
        out_shape=[f32(height, width)] * 2,
        grid=(height // tile,),
        in_specs=[SMEM, SMEM, wide, wide] + [narrow] * (2 * n_rows),
        out_specs=[wide, wide],
        compiler_params=params(60),
        cost_estimate=cost(4e9, 6 * 4 * real.size),
    )(place, hyper, real, imag, *blocks)


def send(values, axis, count, k):
    return lax.ppermute(values, axis, [(i, i ^ k) for i in range(count)])


def exchange(blocks, axis):
    count = len(blocks)
    received = [blocks[0]] + [None] * (count - 1)
    for k in range(count - 1, 0, -1):
        received[k] = send(blocks[k], axis, count, k)
    return received


def sum_over(values, axis, count):
    terms = exchange([values] * count, axis)
    while len(terms) > 1:
        terms = [terms[i] + terms[i + 1] for i in range(0, len(terms), 2)]
    return terms[0]


def tiled_shards(n_rows, n_cols):
    def run(white_real, white_imag, covariates, coefficients, counts, land_mask, field_hyper):
        height, width = white_real.shape
        n_cov = covariates.shape[0]
        my_row, my_col = lax.axis_index("rows"), lax.axis_index("cols")
        place = jnp.stack([my_row, my_row * height, my_col * width, my_col]).astype(jnp.int32)
        spots = jnp.stack([my_row, my_col]).astype(jnp.int32)
        twiddles = jnp.broadcast_to(jnp.asarray(twiddle_table())[:, :, None], (4, DENSE, LANES))
        tables = (jnp.asarray(dense_table()), twiddles)

        partial, squares = (), 0.0
        for j in range(2):
            scaled, part = call_scale(place, field_hyper, white_real, white_imag, n_rows, j)
            squares = squares + part
            if j:
                columns[1], *scaled = lax.optimization_barrier((columns[1], *scaled))
            columns = exchange(scaled, "rows")
            (spread,) = call_first_axis(spots, tables, columns, 1)
            spread = spread.reshape(n_rows * n_cols, LANES, LANES)
            lines = lax.all_to_all(spread, ("rows", "cols"), 0, 0)
            if j:
                latent = list(call_second_axis(spots, tables, lines, partial, n_rows, n_cols))
            else:
                partial = (call_second_axis(spots, tables, lines, partial, n_rows, n_cols),)

        residuals, sums, own, far = [None] * n_cols, 0.0, latent[0], n_cols - 1
        arrived = {0: own, far: send(latent[far], "cols", n_cols, far)}
        for k in range(1, far):
            if k > 1:
                arrived[far], latent[k] = lax.optimization_barrier((arrived[far], latent[k]))
            arrived[k] = send(latent[k], "cols", n_cols, k)
        before = None
        for k in (far, *range(1, far), 0):
            values = arrived[k]
            if before is not None:
                values, _ = lax.optimization_barrier((values, residuals[before]))
            residuals[k], part = call_cell(place, coefficients, values, covariates, counts, land_mask, k)
            sums, before = sums + part, k
        back = [residuals[0]] + [send(residuals[k], "cols", n_cols, k) for k in range(1, n_cols)]
        sums = jnp.sum(sums, axis=(1, 2))
        own_loss = sums[n_cov] + 0.5 * squares
        own = jnp.concatenate([sums[:n_cov], jnp.broadcast_to(own_loss, (LANES - n_cov,))])
        totals = sum_over(sum_over(own, "rows", n_rows), "cols", n_cols)
        spread = call_second_axis_back(spots, tables, back, n_rows, n_cols)
        blocks = []
        for j in range(2):
            lines = lax.all_to_all(spread[j], ("rows", "cols"), 0, 0).reshape(NG, LANES)
            if j:
                lines, *blocks = lax.optimization_barrier((lines, *blocks))
            else:
                lines, totals = lax.optimization_barrier((lines, totals))
            blocks += exchange(call_first_axis(spots, tables, [lines], n_rows), "rows")

        per_cell = 1.0 / (NG * NG)
        coef_grad = (
            totals[:n_cov] * per_cell + lasso_weight * jnp.sign(coefficients) + ridge_weight * coefficients
        )
        objective = (
            totals[n_cov] * per_cell
            + lasso_weight * jnp.sum(jnp.abs(coefficients))
            + 0.5 * ridge_weight * jnp.sum(coefficients * coefficients)
        )
        step_real, step_imag = call_final(place, field_hyper, white_real, white_imag, blocks, n_rows)
        return (step_real, step_imag, coef_grad, objective)

    return run


def field_spectrum(field_hyper, wave_row, wave_col):
    amplitude = 0.2 * field_hyper[0]
    freq_range = field_hyper[1]
    radius = (wave_row[:, None] * wave_row[:, None] + wave_col[None, :] * wave_col[None, :]) / (
        freq_range * freq_range
    )
    return amplitude * (1.0 + NG / freq_range * jnp.power(1.0 + radius, -0.75))


def angle_table(left_len, right_len, modulus):
    product = lax.iota(jnp.int32, left_len)[:, None] * lax.iota(jnp.int32, right_len)[None, :]
    angles = (product % modulus).astype(jnp.float32) * (2.0 * math.pi / modulus)
    return (jnp.cos(angles), jnp.sin(angles))


def inverse_transform(pieces, want_real):
    highest = lax.Precision.HIGHEST
    components = pieces.shape[0]
    row_count = pieces.shape[1]
    length = pieces.shape[2]
    factor = 8
    others = length // factor
    shaped = pieces.reshape(components, row_count, others, factor)
    big_cos, big_sin = angle_table(others, others, others)

    def apply_big(table, block):
        return jnp.einsum("rnm,nk->rmk", block, table, precision=highest)

    if components == 2:
        real_mid = apply_big(big_cos, shaped[0]) - apply_big(big_sin, shaped[1])
        imag_mid = apply_big(big_sin, shaped[0]) + apply_big(big_cos, shaped[1])
    else:
        real_mid = apply_big(big_cos, shaped[0])
        imag_mid = apply_big(big_sin, shaped[0])
    tw_cos, tw_sin = angle_table(factor, others, length)
    real_tw = real_mid * tw_cos - imag_mid * tw_sin
    imag_tw = real_mid * tw_sin + imag_mid * tw_cos
    small_cos, small_sin = angle_table(factor, factor, factor)

    def apply_small(table, block):
        return jnp.einsum("rmk,mj->rjk", block, table, precision=highest)

    real_out = (apply_small(small_cos, real_tw) - apply_small(small_sin, imag_tw)).reshape(
        1, row_count, length
    )
    if want_real:
        return real_out
    imag_out = (apply_small(small_sin, real_tw) + apply_small(small_cos, imag_tw)).reshape(
        1, row_count, length
    )
    return jnp.concatenate([real_out, imag_out], axis=0)


def middle_step(spread):
    returned = lax.all_to_all(spread, "cols", split_axis=2, concat_axis=1, tiled=True)
    flipped = jnp.swapaxes(returned, 1, 2)
    return lax.all_to_all(flipped, "rows", split_axis=1, concat_axis=2, tiled=True)


def grid_transform(pieces, want_real):
    full_rows = lax.all_to_all(pieces, "cols", split_axis=1, concat_axis=2, tiled=True)
    halfway = inverse_transform(full_rows, False)
    columns = middle_step(halfway)
    second = inverse_transform(columns, want_real)
    blocks_out = lax.all_to_all(second, "rows", split_axis=2, concat_axis=1, tiled=True)
    return jnp.swapaxes(blocks_out, 1, 2) * (1.0 / NG)


def shards(white_real, white_imag, covariates, coefficients, counts, land_mask, field_hyper):
    highest = lax.Precision.HIGHEST
    rows_here = white_real.shape[0]
    cols_here = white_real.shape[1]
    freq_row = lax.axis_index("rows") * rows_here + lax.iota(jnp.int32, rows_here)
    freq_col = lax.axis_index("cols") * cols_here + lax.iota(jnp.int32, cols_here)
    wave_row = jnp.minimum(freq_row, NG - freq_row).astype(jnp.float32)
    wave_col = jnp.minimum(freq_col, NG - freq_col).astype(jnp.float32)
    spectrum = field_spectrum(field_hyper, wave_row, wave_col)
    scaled = jnp.stack([spectrum * white_real, spectrum * white_imag])
    latent = grid_transform(scaled, True)[0]
    cov_full = covariates.astype(jnp.float32)
    linear = jnp.einsum("j,jrc->rc", coefficients, cov_full, precision=highest)
    log_rate = linear + latent
    intensity = jnp.exp(log_rate)
    land_vals = land_mask.astype(jnp.float32)
    count_vals = counts.astype(jnp.float32)
    residual = land_vals * (intensity - count_vals)
    partial_coef = jnp.einsum("jrc,rc->j", cov_full, residual, precision=highest)
    partial_loss = jnp.sum(land_vals * (intensity - count_vals * log_rate)) + 0.5 * jnp.sum(
        white_real * white_real + white_imag * white_imag
    )
    adjoint = grid_transform(residual[None], False)
    total_coef, total_loss = lax.psum((partial_coef, partial_loss), ("rows", "cols"))
    per_cell = 1.0 / (NG * NG)
    coef_grad = (
        total_coef * per_cell + lasso_weight * jnp.sign(coefficients) + ridge_weight * coefficients
    )
    objective = (
        total_loss * per_cell
        + lasso_weight * jnp.sum(jnp.abs(coefficients))
        + 0.5 * ridge_weight * jnp.sum(coefficients * coefficients)
    )
    curvature = 1.0 + spectrum * spectrum
    step_real = (spectrum * adjoint[0] + white_real) / curvature
    step_imag = (white_imag - spectrum * adjoint[1]) / curvature
    return (step_real, step_imag, coef_grad, objective)


def solution(mesh):
    n_rows, n_cols = mesh.shape["rows"], mesh.shape["cols"]
    tiled = n_rows * n_cols * LANES == NG and not n_rows & (n_rows - 1) and not n_cols & (n_cols - 1)
    return jax.shard_map(
        tiled_shards(n_rows, n_cols) if tiled else shards,
        mesh=mesh,
        in_specs=(
            P("rows", "cols"),
            P("rows", "cols"),
            P(None, "rows", "cols"),
            P(),
            P("rows", "cols"),
            P("rows", "cols"),
            P(),
        ),
        out_specs=(P("rows", "cols"), P("rows", "cols"), P(), P()),
        check_vma=False,
    )
```

```python
import math

import jax
import jax.numpy as jnp
import ml_dtypes
import numpy as np
from jax import lax
from jax.experimental import pallas as pl
from jax.experimental.pallas import tpu as pltpu
from jax.sharding import PartitionSpec as P

NG = 4096
LANES = 128
HALF = LANES // 2
RADIX = 16
DENSE = NG // RADIX

lasso_weight = 0.02
ridge_weight = 0.1


def split3(values):
    first = values.astype(ml_dtypes.bfloat16)
    rest = values - first.astype(np.float64)
    second = rest.astype(ml_dtypes.bfloat16)
    rest = rest - second.astype(np.float64)
    return first, second, rest.astype(ml_dtypes.bfloat16)


def dense_table():
    index = np.arange(DENSE)
    angles = (index[:, None] * index[None, :] % DENSE) * (2.0 * np.pi / DENSE)
    quarters = index.reshape(4, DENSE // 4)
    columns = [np.concatenate([quarters[j], quarters[j + 2]]) for j in range(2)]
    full = np.concatenate([part[:, at] for at in columns for part in (np.cos(angles), -np.sin(angles))], axis=1)
    return np.concatenate(split3(full), axis=1)


def twiddle_table():
    angles = np.arange(DENSE)[None, :] * np.array([1.0, 4.0])[:, None] * (2.0 * np.pi / NG)
    return np.stack([np.cos(angles[0]), np.sin(angles[0]), np.cos(angles[1]), np.sin(angles[1])]).astype(np.float32)


class Pairs:
    def add(self, a, b):
        return tuple(y if x is None else x if y is None else x + y for x, y in zip(a, b))

    def sub(self, a, b):
        return tuple((None if y is None else -y) if x is None else x if y is None else x - y for x, y in zip(a, b))

    def turn(self, a):
        return (None if a[1] is None else -a[1], a[0])

    def mul(self, a, c, s):
        re, im = a
        if im is None:
            return (re * c, re * s)
        if re is None:
            return (-(im * s), im * c)
        return (re * c - im * s, re * s + im * c)


def dft4(ops, z):
    even, odd = ops.add(z[0], z[2]), ops.sub(z[0], z[2])
    even2, turned = ops.add(z[1], z[3]), ops.turn(ops.sub(z[1], z[3]))
    return [ops.add(even, even2), ops.add(odd, turned), ops.sub(even, even2), ops.sub(odd, turned)]


def dft16(ops, z):
    columns = []
    for q in range(4):
        column = dft4(ops, [z[4 * p + q] for p in range(4)])
        for u in range(1, 4):
            turns = q * u
            if turns == 4:
                column[u] = ops.turn(column[u])
            elif turns:
                angle = 2.0 * math.pi * turns / RADIX
                column[u] = ops.mul(column[u], math.cos(angle), math.sin(angle))
        columns.append(column)
    out = [None] * RADIX
    for u in range(4):
        for v, value in enumerate(dft4(ops, [columns[q][u] for q in range(4)])):
            out[u + 4 * v] = value
    return out


def bf16_parts(values):
    one = values.astype(jnp.bfloat16)
    rest = values - one.astype(jnp.float32)
    two = rest.astype(jnp.bfloat16)
    return [one, two, (rest - two.astype(jnp.float32)).astype(jnp.bfloat16)]


def dense_product(table, first, parts):
    one, two, three = parts
    depth = one.shape[0]

    def dot(part, right):
        start = 2 * DENSE * part + first
        return jnp.dot(table[:, start : start + depth], right, preferred_element_type=jnp.float32)

    small = (dot(2, one) + dot(0, three)) + dot(1, two)
    return (small + (dot(1, one) + dot(0, two))) + dot(0, one)


def powers(twiddle_ref, row, step):
    ops = Pairs()
    w = [None] * RADIX
    at = pl.ds(row, step)
    w[1] = (twiddle_ref[0, at, :], twiddle_ref[1, at, :])
    w[4] = (twiddle_ref[2, at, :], twiddle_ref[3, at, :])
    w[2] = ops.mul(w[1], *w[1])
    w[3] = ops.mul(w[2], *w[1])
    for x in (5, 6, 7):
        w[x] = ops.mul(w[4], *w[x - 4])
    w[8] = ops.mul(w[4], *w[4])
    for x in range(9, RADIX):
        w[x] = ops.mul(w[8], *w[x - 8])
    return w


def butterflies(load, re_ref, im_ref, twiddle_ref, halves=(0, 1)):
    ops = Pairs()
    step = 8
    quarter = DENSE // 4
    for at, j in enumerate(halves):

        def body(i, carry, at=at, j=j):
            slow = i // (quarter // step)
            inner = pl.multiple_of((i % (quarter // step)) * step, step)
            z = dft16(ops, [load(a, 2 * slow + j, inner) for a in range(RADIX)])
            w = powers(twiddle_ref, pl.multiple_of((2 * slow + j) * quarter + inner, step), step)
            for x in range(RADIX):
                re, im = ops.mul(z[x], *w[x]) if x else z[x]
                rows = pl.ds(pl.multiple_of((x * len(halves) + at) * 2 * quarter + i * step, step), step)
                re_ref[rows, :] = re
                im_ref[rows, :] = jnp.zeros((step, LANES), jnp.float32) if im is None else im
            return carry

        lax.fori_loop(0, 2 * quarter // step, body, 0, unroll=4)


def stacked(re_ref, im_ref, x, n_halves):
    half = DENSE // 2
    out = []
    for h in range(n_halves):
        rows = pl.ds(pl.multiple_of((x * n_halves + h) * half, half), half)
        out += [re_ref[rows, :], im_ref[rows, :]]
    return out


def real_products(re_ref, im_ref, table_ref, target, halves=(0, 1)):
    def body(p, carry):
        pair = [jnp.concatenate(stacked(re_ref, im_ref, 2 * p + h, len(halves)), axis=0) for h in range(2)]
        both = dense_product(table_ref, halves[0] * DENSE, bf16_parts(jnp.concatenate(pair, axis=1)))
        for h in range(2):
            target[pl.ds(2 * p + h, DENSE, stride=RADIX), :] = both[:, h * LANES : (h + 1) * LANES]
        return carry

    lax.fori_loop(0, RADIX // 2, body, 0, unroll=4)


def spectrum_of(hyper, first_row, first_col, shape, cols=None):
    rows = lax.broadcasted_iota(jnp.int32, shape, 0) + first_row
    cols = (lax.broadcasted_iota(jnp.int32, shape, 1) if cols is None else cols) + first_col
    wave_row = jnp.minimum(rows, NG - rows).astype(jnp.float32)
    wave_col = jnp.minimum(cols, NG - cols).astype(jnp.float32)
    amplitude = 0.2 * hyper[0]
    span = hyper[1]
    root = lax.rsqrt(1.0 + (wave_row * wave_row + wave_col * wave_col) * (1.0 / (span * span)))
    return amplitude + (amplitude * (NG / span)) * (root * root * lax.rsqrt(root))


def scale_kernel(count, j, place, hyper, real_ref, imag_ref, *outs):
    height = real_ref.shape[0]
    me, first_col = place[0], place[2]
    first_row = place[1] + pl.program_id(0) * height
    lane = lax.broadcasted_iota(jnp.int32, (1, LANES), 1)
    low = lane < HALF
    step = 64
    total = jnp.zeros((8, LANES), jnp.float32)
    for k in range(count):
        start = pl.multiple_of(jnp.bitwise_xor(me, k) * LANES, LANES)
        for row in range(0, height, step):
            real = real_ref[pl.ds(row, step), pl.ds(start, LANES)]
            imag = imag_ref[pl.ds(row, step), pl.ds(start, LANES)]
            squares = real * real + imag * imag
            squares = jnp.where(low, squares, 0.0) if j == 0 else jnp.where(low, 0.0, squares)
            total += jnp.sum(squares.reshape(step // 8, 8, LANES), axis=0)
            if j == 0:
                value = jnp.where(low, real, pltpu.roll(imag, HALF, 1))
            else:
                value = jnp.where(low, pltpu.roll(real, HALF, 1), imag)
            cols = jnp.bitwise_and(lax.broadcasted_iota(jnp.int32, (step, LANES), 1), HALF - 1)
            spec = spectrum_of(hyper, first_row + row, first_col + start + j * HALF, (step, LANES), cols)
            outs[k][pl.ds(row, step), :] = spec * value
    outs[-1][...] = total


def first_axis_kernel(n_in, n_out, place, table_ref, twiddle_ref, *refs):
    ins, outs, (one, two, done) = refs[:n_in], refs[n_in : n_in + n_out], refs[n_in + n_out :]
    me = place[0]
    lane = lax.broadcasted_iota(jnp.int32, (8, LANES), 1)
    sign = jnp.where(lane < HALF, 1.0, -1.0).astype(jnp.float32)
    if n_in > 1:
        height = ins[0].shape[0]
        for k in range(n_in):
            start = pl.multiple_of(jnp.bitwise_xor(me, k) * height, height)
            done[pl.ds(start, height), :] = ins[k][...]
        source = done
    else:
        source = ins[0]
    target = done if n_out > 1 else outs[0]

    def load(a, quarter, inner):
        row = pl.multiple_of(a * DENSE + quarter * (DENSE // 4) + inner, 8)
        value = source[pl.ds(row, 8), :]
        return (value, pltpu.roll(value, HALF, 1) * sign)

    butterflies(load, one, two, twiddle_ref)
    real_products(one, two, table_ref, target)
    if n_out > 1:
        height = outs[0].shape[0]
        for k in range(n_out):
            start = pl.multiple_of(jnp.bitwise_xor(me, k) * height, height)
            outs[k][...] = done[pl.ds(start, height), :]


def second_axis_kernel(n_rows, n_cols, j, place, table_ref, twiddle_ref, *refs):
    lines, refs = refs[0], refs[1:]
    last = j == 1
    if last:
        outs, (real, imag, done, before, arrived) = refs[1 : 1 + n_cols], refs[1 + n_cols :]
        copy = pltpu.make_async_copy(refs[0], before, arrived)
        copy.start()
    else:
        done, real, imag = refs
    me = place[1]
    for r in range(n_rows):
        for c in range(n_cols):
            turned = lines[r * n_cols + c].T
            row = (c * n_rows + r) * HALF
            real[row : row + HALF, :] = turned[:HALF]
            imag[row : row + HALF, :] = turned[HALF:]

    def load(a, quarter, inner):
        rows = pl.ds(pl.multiple_of(2 * a * HALF + (quarter // 2) * HALF + inner, 8), 8)
        return (real[rows, :], imag[rows, :])

    butterflies(load, real, imag, twiddle_ref, (j,))
    real_products(real, imag, table_ref, done, (j,))
    if not last:
        return
    copy.wait()
    width = NG // n_cols
    for k in range(n_cols):
        start = jnp.bitwise_xor(me, k) * width
        rows = pl.ds(pl.multiple_of(start, LANES), width)
        outs[k][...] = done[rows, :] + before[rows, :]


def second_axis_back_kernel(n_rows, n_cols, place, table_ref, twiddle_ref, *refs):
    ins, outs, (real, imag, real_out, imag_out) = refs[:n_cols], refs[n_cols : n_cols + 2], refs[n_cols + 2 :]
    source = real_out
    me = place[1]
    width = NG // n_cols
    for k in range(n_cols):
        start = jnp.bitwise_xor(me, k) * width
        source[pl.ds(pl.multiple_of(start, LANES), width), :] = ins[k][...]

    def load(a, quarter, inner):
        return (source[pl.ds(pl.multiple_of(a * DENSE + quarter * (DENSE // 4) + inner, 8), 8), :], None)

    butterflies(load, real, imag, twiddle_ref)

    def products(x, carry):
        pieces = [bf16_parts(piece) for piece in stacked(real, imag, x, 2)]
        parts = []
        for re0, im0, re1, im1 in zip(*pieces):
            left = jnp.concatenate([re0, im0, re1, im1], axis=0)
            right = jnp.concatenate([im0, -re0, im1, -re1], axis=0)
            parts.append(jnp.concatenate([left, right], axis=1))
        both = dense_product(table_ref, 0, parts)
        rows = pl.ds(x, DENSE, stride=RADIX)
        real_out[rows, :] = both[:, :LANES]
        imag_out[rows, :] = both[:, LANES:]
        return carry

    lax.fori_loop(0, RADIX, products, 0, unroll=4)
    for r in range(n_rows):
        for c in range(n_cols):
            for j in range(2):
                row = (c * n_rows + r) * LANES + j * HALF
                tile = jnp.concatenate([real_out[row : row + HALF, :], imag_out[row : row + HALF, :]], axis=0)
                outs[j][r * n_cols + c] = tile.T


def cell_kernel(n_cov, place, coefficients, latent_ref, cov_ref, counts_ref, mask_ref, residual_ref, sums_ref, values):
    @pl.when(pl.program_id(0) == 0)
    def _():
        sums_ref[...] = jnp.zeros_like(sums_ref)

    width = latent_ref.shape[0]
    step = 16
    for t in range(0, width, LANES):
        values[:, t : t + LANES] = latent_ref[t : t + LANES, :].T

    def fold(value):
        return value[:8] + value[8:]

    for row in range(0, LANES, step):
        rows = slice(row, row + step)

        def body(t, carry, rows=rows):
            lanes = pl.ds(pl.multiple_of(t * LANES, LANES), LANES)
            total = values[rows, lanes] * (1.0 / NG)
            for j in range(n_cov):
                total += coefficients[j] * cov_ref[j, rows, lanes].astype(jnp.float32)
            intensity = jnp.exp(total)
            land = mask_ref[rows, lanes].astype(jnp.float32)
            count = counts_ref[rows, lanes].astype(jnp.float32)
            residual = land * (intensity - count)
            values[rows, lanes] = residual
            for j in range(n_cov):
                sums_ref[j] += fold(cov_ref[j, rows, lanes].astype(jnp.float32) * residual)
            sums_ref[n_cov] += fold(land * (intensity - count * total))
            return carry

        lax.fori_loop(0, width // LANES, body, 0)
    for t in range(0, width, LANES):
        residual_ref[t : t + LANES, :] = values[:, t : t + LANES].T


def final_kernel(count, place, hyper, real_ref, imag_ref, *refs):
    blocks, (step_real_ref, step_imag_ref) = refs[: 2 * count], refs[2 * count :]
    height = real_ref.shape[0]
    me, first_row, first_col = place[0], place[1], place[2]
    lane = lax.broadcasted_iota(jnp.int32, (1, LANES), 1)
    low = lane < HALF
    step = 64
    first_row = first_row + pl.program_id(0) * height
    for at, k in enumerate(far_first(count)):
        start = pl.multiple_of(jnp.bitwise_xor(me, k) * LANES, LANES)
        for row in range(0, height, step):
            rows = pl.ds(row, step)
            lanes = pl.ds(start, LANES)
            spec = spectrum_of(hyper, first_row + row, first_col + start, (step, LANES))
            inverse = 1.0 / (1.0 + spec * spec)
            spec = spec * (1.0 / NG)
            one, two = blocks[at][rows, :], blocks[count + at][rows, :]
            adjoint_real = jnp.where(low, one, pltpu.roll(two, HALF, 1))
            adjoint_imag = jnp.where(low, pltpu.roll(one, HALF, 1), two)
            step_real_ref[rows, lanes] = (spec * adjoint_real + real_ref[rows, lanes]) * inverse
            step_imag_ref[rows, lanes] = (imag_ref[rows, lanes] - spec * adjoint_imag) * inverse


SMEM = pl.BlockSpec(memory_space=pltpu.SMEM)
VMEM = pl.BlockSpec(memory_space=pltpu.VMEM)


def f32(*shape):
    return jax.ShapeDtypeStruct(shape, jnp.float32)


def params(mib):
    return pltpu.CompilerParams(vmem_limit_bytes=mib << 20)


def cost(flops, nbytes):
    return pl.CostEstimate(flops=int(flops), bytes_accessed=int(nbytes), transcendentals=0)


def far_first(count):
    return sorted(range(count), key=lambda k: (-(k >> 1).bit_count(), -(k & 1), k))


def call_scale(place, hyper, real, imag, n_rows, j):
    height, width = real.shape
    tile = 128

    def kernel(*refs):
        scale_kernel(n_rows, j, *refs)

    wide = pl.BlockSpec((tile, width), lambda i: (i, 0))
    narrow = pl.BlockSpec((tile, LANES), lambda i: (i, 0))
    *out, squares = pl.pallas_call(
        kernel,
        name="scale",
        out_shape=[f32(height, LANES)] * n_rows + [f32(8 * height // tile, LANES)],
        grid=(height // tile,),
        in_specs=[SMEM, SMEM, wide, wide],
        out_specs=[narrow] * n_rows + [pl.BlockSpec((8, LANES), lambda i: (i, 0))],
        compiler_params=params(60),
        cost_estimate=cost(2e9, 3 * 4 * real.size),
    )(place, hyper, real, imag)
    return out, jnp.sum(squares)


def call_first_axis(place, tables, ins, n_out):
    n_in = len(ins)

    def kernel(*refs):
        first_axis_kernel(n_in, n_out, *refs)

    return pl.pallas_call(
        kernel,
        name="first_axis",
        out_shape=[f32(NG // n_out, LANES)] * n_out,
        in_specs=[SMEM, VMEM, VMEM] + [VMEM] * n_in,
        out_specs=[VMEM] * n_out,
        scratch_shapes=[pltpu.VMEM((NG, LANES), jnp.float32)] * 3,
        compiler_params=params(32),
        cost_estimate=cost(5e10, 2 * 4 * NG * LANES),
    )(place, *tables, *ins)


def call_second_axis(place, tables, lines, before, n_rows, n_cols):
    j = len(before)

    def kernel(*refs):
        second_axis_kernel(n_rows, n_cols, j, *refs)

    scratch = [pltpu.VMEM((NG // 2, LANES), jnp.float32)] * 2
    return pl.pallas_call(
        kernel,
        name="second_axis",
        out_shape=[f32(NG // n_cols, LANES)] * n_cols if j else f32(NG, LANES),
        in_specs=[SMEM, VMEM, VMEM, VMEM] + [pl.BlockSpec(memory_space=pl.ANY)] * j,
        out_specs=[VMEM] * n_cols if j else VMEM,
        scratch_shapes=scratch + ([pltpu.VMEM((NG, LANES), jnp.float32)] * 2 + [pltpu.SemaphoreType.DMA]) * j,
        compiler_params=params(32),
        cost_estimate=cost(5e10, 3 * 4 * NG * LANES),
    )(place, *tables, lines, *before)


def call_second_axis_back(place, tables, ins, n_rows, n_cols):
    def kernel(*refs):
        second_axis_back_kernel(n_rows, n_cols, *refs)

    return pl.pallas_call(
        kernel,
        name="second_axis_back",
        out_shape=[f32(n_rows * n_cols, LANES, LANES)] * 2,
        in_specs=[SMEM, VMEM, VMEM] + [VMEM] * n_cols,
        out_specs=[VMEM] * 2,
        scratch_shapes=[pltpu.VMEM((NG, LANES), jnp.float32)] * 4,
        compiler_params=params(40),
        cost_estimate=cost(5e10, 3 * 4 * NG * LANES),
    )(place, *tables, *ins)


def call_cell(place, coefficients, latent, covariates, counts, mask, k):
    n_cov = covariates.shape[0]
    width = latent.shape[0]
    tile = 256

    def kernel(*refs):
        cell_kernel(n_cov, *refs)

    def part(i, place, coefficients):
        return (jnp.bitwise_xor(place[3], k), i)

    lines = pl.BlockSpec((tile, LANES), lambda i, p, c: (i, 0))
    return pl.pallas_call(
        kernel,
        name="cell",
        out_shape=[f32(width, LANES), f32(n_cov + 1, 8, LANES)],
        grid_spec=pltpu.PrefetchScalarGridSpec(
            num_scalar_prefetch=2,
            grid=(width // tile,),
            in_specs=[
                lines,
                pl.BlockSpec((n_cov, LANES, tile), lambda i, p, c: (0, *part(i, p, c))),
                pl.BlockSpec((LANES, tile), part),
                pl.BlockSpec((LANES, tile), part),
            ],
            out_specs=[lines, pl.BlockSpec((n_cov + 1, 8, LANES), lambda i, p, c: (0, 0, 0))],
            scratch_shapes=[pltpu.VMEM((LANES, tile), jnp.float32)],
        ),
        compiler_params=params(32),
        cost_estimate=cost(2e10, width * LANES * (2 * n_cov + 16)),
    )(place, coefficients, latent, covariates, counts, mask)


def call_final(place, hyper, real, imag, blocks, n_rows):
    height, width = real.shape
    tile = 128

    def kernel(*refs):
        final_kernel(n_rows, *refs)

    blocks = [blocks[j * n_rows + k] for j in range(2) for k in far_first(n_rows)]
    wide = pl.BlockSpec((tile, width), lambda i: (i, 0))
    narrow = pl.BlockSpec((tile, LANES), lambda i: (i, 0))
    return pl.pallas_call(
        kernel,
        name="final",
        out_shape=[f32(height, width)] * 2,
        grid=(height // tile,),
        in_specs=[SMEM, SMEM, wide, wide] + [narrow] * (2 * n_rows),
        out_specs=[wide, wide],
        compiler_params=params(60),
        cost_estimate=cost(4e9, 6 * 4 * real.size),
    )(place, hyper, real, imag, *blocks)


def send(values, axis, count, k):
    return lax.ppermute(values, axis, [(i, i ^ k) for i in range(count)])


def exchange(blocks, axis):
    count = len(blocks)
    received = [blocks[0]] + [None] * (count - 1)
    for k in range(count - 1, 0, -1):
        received[k] = send(blocks[k], axis, count, k)
    return received


def sum_over(values, axis, count):
    terms = exchange([values] * count, axis)
    while len(terms) > 1:
        terms = [terms[i] + terms[i + 1] for i in range(0, len(terms), 2)]
    return terms[0]


def tiled_shards(n_rows, n_cols):
    def run(white_real, white_imag, covariates, coefficients, counts, land_mask, field_hyper):
        height, width = white_real.shape
        n_cov = covariates.shape[0]
        my_row, my_col = lax.axis_index("rows"), lax.axis_index("cols")
        place = jnp.stack([my_row, my_row * height, my_col * width, my_col]).astype(jnp.int32)
        spots = jnp.stack([my_row, my_col]).astype(jnp.int32)
        twiddles = jnp.broadcast_to(jnp.asarray(twiddle_table())[:, :, None], (4, DENSE, LANES))
        tables = (jnp.asarray(dense_table()), twiddles)

        partial, squares = (), 0.0
        for j in range(2):
            scaled, part = call_scale(place, field_hyper, white_real, white_imag, n_rows, j)
            squares = squares + part
            if j:
                columns[1], *scaled = lax.optimization_barrier((columns[1], *scaled))
            columns = exchange(scaled, "rows")
            (spread,) = call_first_axis(spots, tables, columns, 1)
            spread = spread.reshape(n_rows * n_cols, LANES, LANES)
            lines = lax.all_to_all(spread, ("rows", "cols"), 0, 0)
            if j:
                latent = list(call_second_axis(spots, tables, lines, partial, n_rows, n_cols))
            else:
                partial = (call_second_axis(spots, tables, lines, partial, n_rows, n_cols),)

        latent = exchange(latent, "cols")
        residuals, sums = [], 0.0
        for k in range(n_cols):
            residual, part = call_cell(place, coefficients, latent[k], covariates, counts, land_mask, k)
            residuals.append(residual)
            sums = sums + part
        back = exchange(residuals, "cols")
        sums = jnp.sum(sums, axis=(1, 2))
        own_loss = sums[n_cov] + 0.5 * squares
        own = jnp.concatenate([sums[:n_cov], jnp.broadcast_to(own_loss, (LANES - n_cov,))])
        totals = sum_over(sum_over(own, "rows", n_rows), "cols", n_cols)
        spread = call_second_axis_back(spots, tables, back, n_rows, n_cols)
        blocks = []
        for j in range(2):
            lines = lax.all_to_all(spread[j], ("rows", "cols"), 0, 0).reshape(NG, LANES)
            if j:
                lines, *blocks = lax.optimization_barrier((lines, *blocks))
            else:
                lines, totals = lax.optimization_barrier((lines, totals))
            blocks += exchange(call_first_axis(spots, tables, [lines], n_rows), "rows")

        per_cell = 1.0 / (NG * NG)
        coef_grad = (
            totals[:n_cov] * per_cell + lasso_weight * jnp.sign(coefficients) + ridge_weight * coefficients
        )
        objective = (
            totals[n_cov] * per_cell
            + lasso_weight * jnp.sum(jnp.abs(coefficients))
            + 0.5 * ridge_weight * jnp.sum(coefficients * coefficients)
        )
        step_real, step_imag = call_final(place, field_hyper, white_real, white_imag, blocks, n_rows)
        return (step_real, step_imag, coef_grad, objective)

    return run


def field_spectrum(field_hyper, wave_row, wave_col):
    amplitude = 0.2 * field_hyper[0]
    freq_range = field_hyper[1]
    radius = (wave_row[:, None] * wave_row[:, None] + wave_col[None, :] * wave_col[None, :]) / (
        freq_range * freq_range
    )
    return amplitude * (1.0 + NG / freq_range * jnp.power(1.0 + radius, -0.75))


def angle_table(left_len, right_len, modulus):
    product = lax.iota(jnp.int32, left_len)[:, None] * lax.iota(jnp.int32, right_len)[None, :]
    angles = (product % modulus).astype(jnp.float32) * (2.0 * math.pi / modulus)
    return (jnp.cos(angles), jnp.sin(angles))


def inverse_transform(pieces, want_real):
    highest = lax.Precision.HIGHEST
    components = pieces.shape[0]
    row_count = pieces.shape[1]
    length = pieces.shape[2]
    factor = 8
    others = length // factor
    shaped = pieces.reshape(components, row_count, others, factor)
    big_cos, big_sin = angle_table(others, others, others)

    def apply_big(table, block):
        return jnp.einsum("rnm,nk->rmk", block, table, precision=highest)

    if components == 2:
        real_mid = apply_big(big_cos, shaped[0]) - apply_big(big_sin, shaped[1])
        imag_mid = apply_big(big_sin, shaped[0]) + apply_big(big_cos, shaped[1])
    else:
        real_mid = apply_big(big_cos, shaped[0])
        imag_mid = apply_big(big_sin, shaped[0])
    tw_cos, tw_sin = angle_table(factor, others, length)
    real_tw = real_mid * tw_cos - imag_mid * tw_sin
    imag_tw = real_mid * tw_sin + imag_mid * tw_cos
    small_cos, small_sin = angle_table(factor, factor, factor)

    def apply_small(table, block):
        return jnp.einsum("rmk,mj->rjk", block, table, precision=highest)

    real_out = (apply_small(small_cos, real_tw) - apply_small(small_sin, imag_tw)).reshape(
        1, row_count, length
    )
    if want_real:
        return real_out
    imag_out = (apply_small(small_sin, real_tw) + apply_small(small_cos, imag_tw)).reshape(
        1, row_count, length
    )
    return jnp.concatenate([real_out, imag_out], axis=0)


def middle_step(spread):
    returned = lax.all_to_all(spread, "cols", split_axis=2, concat_axis=1, tiled=True)
    flipped = jnp.swapaxes(returned, 1, 2)
    return lax.all_to_all(flipped, "rows", split_axis=1, concat_axis=2, tiled=True)


def grid_transform(pieces, want_real):
    full_rows = lax.all_to_all(pieces, "cols", split_axis=1, concat_axis=2, tiled=True)
    halfway = inverse_transform(full_rows, False)
    columns = middle_step(halfway)
    second = inverse_transform(columns, want_real)
    blocks_out = lax.all_to_all(second, "rows", split_axis=2, concat_axis=1, tiled=True)
    return jnp.swapaxes(blocks_out, 1, 2) * (1.0 / NG)


def shards(white_real, white_imag, covariates, coefficients, counts, land_mask, field_hyper):
    highest = lax.Precision.HIGHEST
    rows_here = white_real.shape[0]
    cols_here = white_real.shape[1]
    freq_row = lax.axis_index("rows") * rows_here + lax.iota(jnp.int32, rows_here)
    freq_col = lax.axis_index("cols") * cols_here + lax.iota(jnp.int32, cols_here)
    wave_row = jnp.minimum(freq_row, NG - freq_row).astype(jnp.float32)
    wave_col = jnp.minimum(freq_col, NG - freq_col).astype(jnp.float32)
    spectrum = field_spectrum(field_hyper, wave_row, wave_col)
    scaled = jnp.stack([spectrum * white_real, spectrum * white_imag])
    latent = grid_transform(scaled, True)[0]
    cov_full = covariates.astype(jnp.float32)
    linear = jnp.einsum("j,jrc->rc", coefficients, cov_full, precision=highest)
    log_rate = linear + latent
    intensity = jnp.exp(log_rate)
    land_vals = land_mask.astype(jnp.float32)
    count_vals = counts.astype(jnp.float32)
    residual = land_vals * (intensity - count_vals)
    partial_coef = jnp.einsum("jrc,rc->j", cov_full, residual, precision=highest)
    partial_loss = jnp.sum(land_vals * (intensity - count_vals * log_rate)) + 0.5 * jnp.sum(
        white_real * white_real + white_imag * white_imag
    )
    adjoint = grid_transform(residual[None], False)
    total_coef, total_loss = lax.psum((partial_coef, partial_loss), ("rows", "cols"))
    per_cell = 1.0 / (NG * NG)
    coef_grad = (
        total_coef * per_cell + lasso_weight * jnp.sign(coefficients) + ridge_weight * coefficients
    )
    objective = (
        total_loss * per_cell
        + lasso_weight * jnp.sum(jnp.abs(coefficients))
        + 0.5 * ridge_weight * jnp.sum(coefficients * coefficients)
    )
    curvature = 1.0 + spectrum * spectrum
    step_real = (spectrum * adjoint[0] + white_real) / curvature
    step_imag = (white_imag - spectrum * adjoint[1]) / curvature
    return (step_real, step_imag, coef_grad, objective)


def solution(mesh):
    n_rows, n_cols = mesh.shape["rows"], mesh.shape["cols"]
    tiled = n_rows * n_cols * LANES == NG and not n_rows & (n_rows - 1) and not n_cols & (n_cols - 1)
    return jax.shard_map(
        tiled_shards(n_rows, n_cols) if tiled else shards,
        mesh=mesh,
        in_specs=(
            P("rows", "cols"),
            P("rows", "cols"),
            P(None, "rows", "cols"),
            P(),
            P("rows", "cols"),
            P("rows", "cols"),
            P(),
        ),
        out_specs=(P("rows", "cols"), P("rows", "cols"), P(), P()),
        check_vma=False,
    )
```
